512 devices in a mesh: seq: 4 (over y_lo, core), head: 8 (over x, y_hi), dp: 16 (over z).
Axes of the slice: x: 4, y: 4 (y_hi: 2, y_lo: 2; y = y_hi * 2 + y_lo), z: 16, core: 2. Of those that a mesh axis runs over, the one named last changes fastest.
Arguments:
- queries: bfloat16 [16, 2048, 4096], P('dp', 'seq', 'head'), may hold values from -2 to 2
- keys: bfloat16 [16, 2048, 4096], P('dp', 'seq', 'head'), may hold values from -2 to 2
- values: bfloat16 [16, 2048, 4096], P('dp', 'seq', 'head'), may hold values from -6 to 6
- out_proj: bfloat16 [4096, 1024], P('head', 'dp'), may hold values from -0.09375 to 0.09375
- depth_proj: bfloat16 [1024, 1024], P(None, ('head', 'dp')), may hold values from -0.1875 to 0.1875
- code_table: bfloat16 [2, 1024, 1024], P(None, ('head', 'dp')), may hold values from -6 to 6
- code_ids: int32 [16, 2048, 2], P('dp', ('seq', 'head')), may hold values from 0 to 1023
- depth_cotangent: bfloat16 [16, 2048, 2, 1024], P('dp', ('seq', 'head')), may hold values from -6 to 6
Outputs:
- grad_queries: bfloat16 [16, 2048, 4096], P('dp', 'seq', 'head')
- grad_keys: bfloat16 [16, 2048, 4096], P('dp', 'seq', 'head')
- grad_values: bfloat16 [16, 2048, 4096], P('dp', 'seq', 'head')
- grad_out_proj: float32 [4096, 1024], P('head', 'dp')
The draws below stay inside these ranges and needn't reach their ends.
All inputs are finite; a program needn't handle non-finite values.
Results may differ from the reference program's by a relative error of at most 0.024.
Values may be sent and summed in bfloat16 or wider, within the bound.
A program may use at most 64 MiB of HBM per device.

```python
import jax
import jax.numpy as jnp
from jax import lax

DH = 128
DW = 1024
VOCAB = 1024
LEVELS = 2
GROUP = 512
HEADS = 32
LENGTH = 2048
BATCH = 16
N_SEQ = 4


def place_ends(drawn, stream_key, low, largest):
    longest = drawn.shape.index(max(drawn.shape))
    spots = []
    for shift in (0, 1):
        where = [jax.random.randint(jax.random.fold_in(stream_key, axis), (), 0, length) for axis, length in enumerate(drawn.shape)]
        where[longest] = (where[longest] + shift) % drawn.shape[longest]
        spots.append(tuple(where))
    return drawn.at[spots[0]].set(low).at[spots[1]].set(largest)


def levels(own_key, shape, split, smallest, top_value):
    loudness = 1.0
    for dim, shards_of in split:
        draws = jax.random.uniform(jax.random.fold_in(jax.random.fold_in(own_key, 6), dim), (shards_of,), jnp.float32, smallest / len(split), top_value / len(split))
        loudness = loudness * jnp.repeat(jnp.exp(draws), shape[dim] // shards_of).reshape((-1,) + (1,) * (len(shape) - 1 - dim))
    return loudness


def scatter_about(stream_key, shape, deviation, most, cuts=(), kind=jnp.bfloat16):
    factor_of = levels(stream_key, shape, cuts, -0.22, 0.18) if cuts else 1.0
    array = jax.random.normal(stream_key, shape, jnp.float32) * deviation * factor_of
    return jnp.minimum(jnp.maximum(array, -most), most).astype(kind)


def setup_inputs(seed: int = 0) -> dict:
    seeds = jax.random.split(jax.random.key(seed), 9)
    return {
        "queries": scatter_about(seeds[0], (BATCH, LENGTH, HEADS * DH), 0.3, 2.0, ((0, 16), (1, 4), (2, 8))),
        "keys": scatter_about(seeds[1], (BATCH, LENGTH, HEADS * DH), 0.3, 2.0, ((0, 16), (1, 4), (2, 8))),
        "values": scatter_about(seeds[2], (BATCH, LENGTH, HEADS * DH), 1.0, 6.0, ((0, 16), (1, 4), (2, 8))),
        "out_proj": scatter_about(seeds[3], (HEADS * DH, DW), (HEADS * DH) ** -0.5, 0.09375, ((0, 8), (1, 16))),
        "depth_proj": scatter_about(seeds[4], (DW, DW), DW ** -0.5, 0.1875, ((1, 128),)),
        "code_table": scatter_about(seeds[5], (LEVELS, VOCAB, DW), 1.0, 6.0, ((1, 128),)),
        "code_ids": place_ends(jax.random.randint(seeds[6], (BATCH, LENGTH, LEVELS), 0, VOCAB), jax.random.fold_in(seeds[6], 1), 0, VOCAB - 1).astype(jnp.int32),
        "depth_cotangent": scatter_about(seeds[7], (BATCH, LENGTH, LEVELS, DW), 1.0, 6.0, ((0, 16), (1, 32))),
    }


def causal_mask(size):
    places = jnp.arange(size, dtype=jnp.int32)
    return (places[:, None] >= places[None, :]).astype(jnp.float32)

def depth_forward(carried, code_tab, proj_mat, code_rows):
    vocab_idx = jnp.arange(code_tab.shape[1], dtype=jnp.int32)
    level_outs = []
    for level_idx in range(code_tab.shape[0]):
        onehot = (code_rows[:, level_idx][:, None] == vocab_idx[None, :]).astype(jnp.bfloat16)
        embedded = jnp.dot(onehot, code_tab[level_idx], preferred_element_type=jnp.float32)
        summed = carried + embedded
        normed = (summed * lax.rsqrt(lax.optimization_barrier(jnp.mean(summed * summed, axis=-1, keepdims=True)) + 1e-05)).astype(jnp.bfloat16)
        projected = jnp.dot(normed, proj_mat, preferred_element_type=jnp.float32)
        level_outs.append(projected)
        carried = summed + jax.nn.silu(projected)
    return jnp.stack(level_outs, axis=1)

def depth_grad(rows_in, code_tab, proj_mat, code_rows, cotangent):
    _, pullback = jax.vjp(lambda inputs: depth_forward(inputs, code_tab, proj_mat, code_rows), rows_in)
    return pullback(cotangent.astype(jnp.float32))[0]

def exclusive(stack, backward):
    if backward:
        running = jnp.cumsum(stack[::-1], axis=0)[::-1]
        return jnp.concatenate([running[1:], jnp.zeros_like(stack[:1])], axis=0)
    running = jnp.cumsum(stack, axis=0)
    return jnp.concatenate([jnp.zeros_like(stack[:1]), running[:-1]], axis=0)

def bf_round(value):
    return lax.optimization_barrier(value.astype(jnp.bfloat16)).astype(jnp.float32)

def reference(queries, keys, values, out_proj, depth_proj, code_table, code_ids, depth_cotangent):
    att_scale = float(LENGTH) ** (-0.5)
    head_count = queries.shape[2] // DH
    causal = causal_mask(GROUP)
    shape_four = (N_SEQ, GROUP, head_count, DH)

    def per_sequence(packed):
        query_seq, key_seq, value_seq, code_rows, cotangent = packed
        query_f = query_seq.reshape(shape_four).astype(jnp.float32)
        key_f = key_seq.reshape(shape_four).astype(jnp.float32)
        value_f = value_seq.reshape(shape_four).astype(jnp.float32)
        state_local = jnp.einsum('nchd,nche->nhde', key_f, value_f)
        state_in = bf_round(exclusive(state_local, False))
        scores = bf_round(jnp.einsum('nthd,nshd->nhts', query_f, key_f) * causal)
        attended = (att_scale * (jnp.einsum('nhts,nshe->nthe', scores, value_f) + jnp.einsum('nthd,nhde->nthe', query_f, state_in))).astype(jnp.bfloat16)
        attended_flat = attended.reshape(LENGTH, head_count * DH)
        mixed = jnp.dot(attended_flat, out_proj, preferred_element_type=jnp.float32)
        grad_mixed = depth_grad(mixed, code_table, depth_proj, code_rows, cotangent).astype(jnp.bfloat16)
        grad_att = jnp.dot(grad_mixed, out_proj.T, preferred_element_type=jnp.float32).astype(jnp.bfloat16)
        weight_term = jnp.dot(attended_flat.T, grad_mixed, preferred_element_type=jnp.float32)
        grad_f = grad_att.reshape(shape_four).astype(jnp.float32)
        back_state = bf_round(exclusive(jnp.einsum('nthd,nthe->nhde', query_f, grad_f), True))
        grad_scores = bf_round(jnp.einsum('nthe,nshe->nhts', grad_f, value_f) * causal)
        grad_query = att_scale * (jnp.einsum('nhts,nshd->nthd', grad_scores, key_f) + jnp.einsum('nthe,nhde->nthd', grad_f, state_in))
        grad_key = att_scale * (jnp.einsum('nhts,nthd->nshd', grad_scores, query_f) + jnp.einsum('nshe,nhde->nshd', value_f, back_state))
        grad_value = att_scale * (jnp.einsum('nhts,nthe->nshe', scores, grad_f) + jnp.einsum('nshd,nhde->nshe', key_f, back_state))
        return (grad_query.reshape(LENGTH, head_count * DH).astype(jnp.bfloat16), grad_key.reshape(LENGTH, head_count * DH).astype(jnp.bfloat16), grad_value.reshape(LENGTH, head_count * DH).astype(jnp.bfloat16), weight_term)
    results = lax.map(per_sequence, (queries, keys, values, code_ids, depth_cotangent))
    return (results[0], results[1], results[2], lax.optimization_barrier(jnp.sum(results[3], axis=0)))
```

```python
import functools

import jax
import jax.numpy as jnp
from jax import lax
from jax.experimental import pallas as pl
from jax.experimental.pallas import tpu as pltpu
from jax.sharding import PartitionSpec as P

DH = 128
F32 = jnp.float32
BF16 = jnp.bfloat16
EPS = 1e-05
HALF = 256
N_COPIES = 200


def dot(a, b):
    return lax.dot_general(a, b, (((1,), (0,)), ((), ())), preferred_element_type=F32)


def dot_nt(a, b):
    return lax.dot_general(a, b, (((1,), (1,)), ((), ())), preferred_element_type=F32)


def dot_tn(a, b):
    return lax.dot_general(a, b, (((0,), (0,)), ((), ())), preferred_element_type=F32)


class Copies:
    def __init__(self, send_sems, recv_sems):
        self.send_sems, self.recv_sems, self.all = send_sems, recv_sems, []

    def send(self, src, dst, device):
        index = len(self.all)
        copy = pltpu.make_async_remote_copy(
            src_ref=src,
            dst_ref=dst,
            send_sem=self.send_sems.at[index],
            recv_sem=self.recv_sems.at[index],
            device_id=device,
            device_id_type=pl.DeviceIdType.MESH,
        )
        copy.start()
        self.all.append(copy)
        return copy

    def drain(self):
        for copy in self.all:
            copy.wait_send()


def kernel(
    scale,
    q_ref, k_ref, v_ref, op_ref, wp_ref, ids_ref, cot_ref,
    gq_ref, gk_ref, gv_ref, go_ref,
    wz, proj, wts,
    s_own, s_recv, t_own, t_recv, s_in,
    b_own, b_recv, bt_own, bt_recv, b_in,
    sc, acc, att,
    mix, ra1, rb1, ra2, rb2, ray, rar, raf, rbr, rbf, yb, sb1, sb2,
    mixed, emb, gpre,
    gb, gra, grb,
    ga, wg, wgr, zsend_r, zrecv_r, zsend_l, zrecv_l, y_own, y_recv, o_own, o_recv,
    send_sems, recv_sems,
):
    seq, head, z = lax.axis_index("seq"), lax.axis_index("head"), lax.axis_index("dp")
    x, yh, yl, c = head // 2, head % 2, seq // 2, seq % 2
    y = 2 * yh + yl
    nz = 16

    def at_x(step):
        return (x + step + 4) % 4

    def at_y(step):
        return (y + step + 4) % 4

    def at_z(step):
        return (z + step + nz) % nz

    def dev(x_=None, y_=None, z_=None, c_=None):
        x_ = x if x_ is None else x_
        y_ = y if y_ is None else y_
        z_ = z if z_ is None else z_
        c_ = c if c_ is None else c_
        return {"seq": 2 * (y_ % 2) + c_, "head": 2 * x_ + y_ // 2, "dp": z_}

    xp, xm = dev(x_=at_x(1)), dev(x_=at_x(-1))
    yp, ym = dev(y_=at_y(1)), dev(y_=at_y(-1))
    zp, zm = dev(z_=at_z(1)), dev(z_=at_z(-1))
    mate = dev(c_=1 - c)
    pair = dev(y_=2 * yh + 1 - yl)
    cf, ylf = c.astype(F32), yl.astype(F32)
    go = Copies(send_sems, recv_sems)

    barrier = pltpu.get_barrier_semaphore()
    for other in (xp, xm, yp, ym, zp, zm, mate):
        pl.semaphore_signal(barrier, inc=1, device_id=other, device_id_type=pl.DeviceIdType.MESH)

    def hs(i):
        return slice(i * DH, (i + 1) * DH)

    for i in range(4):
        s_own[i] = dot_tn(k_ref[:, hs(i)], v_ref[:, hs(i)]).astype(BF16)
    pl.semaphore_wait(barrier, 7)

    quarter = 2 * c + yl
    mine = c * 32

    state_copy = go.send(s_own, s_recv, mate)
    own_w = wp_ref.at[quarter]
    own_p = op_ref.at[pl.ds(pl.multiple_of(mine, 32), 32), :]

    def w_slot(j):
        return wz.at[j]

    def p_slot(j):
        return proj.at[j, c]

    wr = go.send(own_w, w_slot(z), zp)
    wl = go.send(own_w, w_slot(z), zm)
    pr = go.send(own_p, p_slot(z), zp)
    pll = go.send(own_p, p_slot(z), zm)
    wz[z] = wp_ref[quarter]
    proj[z] = op_ref[...].reshape(2, 32, 512)

    rows = lax.broadcasted_iota(jnp.int32, (HALF, HALF), 0)
    cols = lax.broadcasted_iota(jnp.int32, (HALF, HALF), 1)
    low = rows >= cols
    top, bot = slice(0, HALF), slice(HALF, 2 * HALF)

    def scores_of(a_ref, b_ref, i):
        a0, a1 = a_ref[top, hs(i)], a_ref[bot, hs(i)]
        b0, b1 = b_ref[top, hs(i)], b_ref[bot, hs(i)]
        m00 = jnp.where(low, dot_nt(a0, b0), 0.0).astype(BF16)
        m10 = dot_nt(a1, b0).astype(BF16)
        m11 = jnp.where(low, dot_nt(a1, b1), 0.0).astype(BF16)
        return m00, m10, m11

    def forward(i):
        m00, m10, m11 = scores_of(q_ref, k_ref, i)
        sc[i, 0], sc[i, 1], sc[i, 2] = m00, m10, m11
        v0, v1 = v_ref[top, hs(i)], v_ref[bot, hs(i)]
        acc[top, hs(i)] = dot(m00, v0)
        acc[bot, hs(i)] = dot(m10, v0) + dot(m11, v1)

    def pass_state():
        state_copy.wait_recv()
        t_own[...] = (s_own[...].astype(F32) + s_recv[...].astype(F32)).astype(BF16)
        return go.send(t_own, t_recv, pair)

    def finish_attended():
        pair_copy.wait_recv()
        s_in[...] = (cf * s_recv[...].astype(F32) + ylf * t_recv[...].astype(F32)).astype(BF16)
        for i in range(4):
            att[:, hs(i)] = (
                scale * (acc[:, hs(i)] + dot(q_ref[:, hs(i)], s_in[i]))
            ).astype(BF16)

    pair_copy = None
    to_mate = []
    for step in range(1, 9):
        wr.wait_recv()
        if step < 8:
            src = at_z(-step)
            wr = go.send(w_slot(src), w_slot(src), zp)
            wl.wait_recv()
        if step < 7:
            src = at_z(step)
            wl = go.send(w_slot(src), w_slot(src), zm)
        pr.wait_recv()
        src = at_z(-step)
        if step < 8:
            pr = go.send(p_slot(src), p_slot(src), zp)
        to_mate.append(go.send(p_slot(src), p_slot(src), mate))
        if step < 8:
            pll.wait_recv()
            src = at_z(step)
            if step < 7:
                pll = go.send(p_slot(src), p_slot(src), zm)
            to_mate.append(go.send(p_slot(src), p_slot(src), mate))
        if step == 1:
            pair_copy = pass_state()
        if step <= 4:
            forward(step - 1)
        if step == 5:
            finish_attended()

    q0 = pl.multiple_of(quarter * 256, 256)
    c0 = pl.multiple_of(c * 512, 512)
    for a in range(3):
        for hf in range(2):
            block = wz[hf * 8:hf * 8 + 8, a].astype(F32)
            piece = jnp.concatenate(
                [block[:, :8].reshape(64, 128), block[:, 8:].reshape(64, 128)], axis=1
            )
            wts[a, x, yh, hf, :, pl.ds(q0, 256)] = piece.astype(BF16)

    def qcols(y_):
        return pl.ds(pl.multiple_of((2 * c + y_ % 2) * 256, 256), 256)

    ccols = pl.ds(c0, 512)

    def send_w(win, device):
        return go.send(win, win, device)

    def wa_x(xx, r0=0, n=64):
        return wts.at[:, xx, yh, 0, pl.ds(r0, n), qcols(y)]

    def wb_y(yy, r0=0, n=64):
        return wts.at[:, x, yy // 2, 1, pl.ds(r0, n), qcols(yy)]

    def wa_y(a, yy, r0=0, n=64):
        return wts.at[a, :, yy // 2, 0, pl.ds(r0, n), qcols(yy)]

    def wb_x(a, xx, r0=0, n=64):
        return wts.at[a, xx, :, 1, pl.ds(r0, n), ccols]

    wax_p, wax_m = send_w(wa_x(x), xp), send_w(wa_x(x), xm)
    wby_p, wby_m = send_w(wb_y(y), yp), send_w(wb_y(y), ym)

    for copy in to_mate:
        copy.wait_recv()

    def mix_block(j):
        part = dot_nt(att[...], proj[4 * j:4 * j + 4].reshape(256, 512))
        mix[:, :, :, :, 256 * j:256 * j + 256] = part.astype(BF16).reshape(4, 2, 2, 32, 256)

    al, be = slice(0, 512), slice(512, 1024)
    mix_block(2)
    mix_block(3)
    mby_p = go.send(mix.at[:, 1 - yh, 0, :, pl.ds(512, 512)], rbr.at[0], yp)
    mby_m = go.send(mix.at[:, 1 - yh, 1, :, pl.ds(512, 512)], rbr.at[1], ym)
    mix_block(0)
    mix_block(1)
    max_p = go.send(mix.at[at_x(2), 0, :, :, pl.ds(0, 512)], ra1, xp)
    max_m = go.send(mix.at[at_x(2), 1, :, :, pl.ds(0, 512)], rb1, xm)

    wax_p.wait_recv()
    wax_m.wait_recv()
    wax2_p = send_w(wa_x(at_x(-1), 0, 32), xp)
    wax2_m = send_w(wa_x(at_x(1), 32, 32), xm)
    wby_p.wait_recv()
    wby_m.wait_recv()
    wby2_p = send_w(wb_y(at_y(-1), 0, 32), yp)
    wby2_m = send_w(wb_y(at_y(1), 32, 32), ym)

    mby_p.wait_recv()
    mby_m.wait_recv()
    mbf_p = go.send(rbr.at[0], rbf.at[0], yp)
    mbf_m = go.send(rbr.at[1], rbf.at[1], ym)
    max_p.wait_recv()
    max_m.wait_recv()
    mix[at_x(1), 0, :, :, al] = (
        mix[at_x(1), 0, :, :, al].astype(F32) + ra1[...].astype(F32)
    ).astype(BF16)
    mix[at_x(-1), 1, :, :, al] = (
        mix[at_x(-1), 1, :, :, al].astype(F32) + rb1[...].astype(F32)
    ).astype(BF16)
    max2_p = go.send(mix.at[at_x(1), :, :, :, pl.ds(0, 512)], ra2, xp)
    max2_m = go.send(mix.at[at_x(-1), :, :, :, pl.ds(0, 512)], rb2, xm)

    wax2_p.wait_recv()
    wax2_m.wait_recv()
    wby2_p.wait_recv()
    wby2_m.wait_recv()
    way, wbx = [None] * 3, [None] * 3
    w_mate = []

    def bulk(a):
        way[a] = (send_w(wa_y(a, y), yp), send_w(wa_y(a, y), ym))
        wbx[a] = (send_w(wb_x(a, x), xp), send_w(wb_x(a, x), xm))
        w_mate.append(send_w(wa_y(a, y), mate))
        w_mate.append(send_w(wb_x(a, x), mate))

    way2, wbx2 = [None] * 3, [None] * 3

    def bulk_relay(a):
        for copy in way[a] + wbx[a]:
            copy.wait_recv()
        way2[a] = (
            send_w(wa_y(a, at_y(-1), 0, 32), yp),
            send_w(wa_y(a, at_y(1), 32, 32), ym),
        )
        wbx2[a] = (
            send_w(wb_x(a, at_x(-1), 0, 32), xp),
            send_w(wb_x(a, at_x(1), 32, 32), xm),
        )
        w_mate.append(send_w(wa_y(a, at_y(-1)), mate))
        w_mate.append(send_w(wa_y(a, at_y(1)), mate))
        w_mate.append(send_w(wb_x(a, at_x(-1)), mate))
        w_mate.append(send_w(wb_x(a, at_x(1)), mate))

    def bulk_end(a):
        for copy in way2[a] + wbx2[a]:
            copy.wait_recv()
        w_mate.append(send_w(wa_y(a, at_y(2)), mate))
        w_mate.append(send_w(wb_x(a, at_x(2)), mate))

    bulk(1)
    mbf_p.wait_recv()
    mbf_m.wait_recv()
    for hf in range(2):
        yb[:, hf] = (
            mix[:, yh, hf, :, be].astype(F32) + rbf[hf].astype(F32)
        ).astype(BF16)
    mbx_p = go.send(yb.at[at_x(2), 0], sb1.at[0], xp)
    mbx_m = go.send(yb.at[at_x(2), 1], sb1.at[1], xm)
    max2_p.wait_recv()
    max2_m.wait_recv()
    ray[...] = (
        mix[x, 1 - yh, :, :, al].astype(F32)
        + ra2[1 - yh].astype(F32)
        + rb2[1 - yh].astype(F32)
    ).astype(BF16)
    may_p = go.send(ray.at[0], rar.at[0], yp)
    may_m = go.send(ray.at[1], rar.at[1], ym)
    mixed[:, al] = (
        mix[x, yh, :, :, al].astype(F32) + ra2[yh].astype(F32) + rb2[yh].astype(F32)
    ).reshape(64, 512)
    bulk(0)
    mbx_p.wait_recv()
    mbx_m.wait_recv()
    yb[at_x(1), 0] = (yb[at_x(1), 0].astype(F32) + sb1[0].astype(F32)).astype(BF16)
    yb[at_x(-1), 1] = (yb[at_x(-1), 1].astype(F32) + sb1[1].astype(F32)).astype(BF16)
    mbx2_p = go.send(yb.at[at_x(1)], sb2.at[0], xp)
    mbx2_m = go.send(yb.at[at_x(-1)], sb2.at[1], xm)
    may_p.wait_recv()
    may_m.wait_recv()
    maf_p = go.send(rar.at[0], raf.at[0], yp)
    maf_m = go.send(rar.at[1], raf.at[1], ym)
    bulk(2)
    bulk_relay(1)
    maf_p.wait_recv()
    maf_m.wait_recv()
    mixed[:, al] = mixed[:, al] + raf[...].astype(F32).reshape(64, 512)
    mbx2_p.wait_recv()
    mbx2_m.wait_recv()
    mixed[:, be] = (
        yb[x].astype(F32) + sb2[0].astype(F32) + sb2[1].astype(F32)
    ).reshape(64, 512)
    bulk_relay(0)
    bulk_end(1)
    bulk_relay(2)
    bulk_end(0)
    bulk_end(2)
    for copy in w_mate:
        copy.wait_recv()

    def weight(a, xx):
        return wts[a, xx].reshape(256, 1024)

    vocab = lax.broadcasted_iota(jnp.int32, (64, 1024), 1)
    for level in range(2):
        onehot = jnp.where(ids_ref[:, level:level + 1] == vocab, 1.0, 0.0).astype(BF16)
        total = None
        for xx in range(4):
            term = dot(onehot[:, 256 * xx:256 * xx + 256], weight(1 + level, xx))
            total = term if total is None else total + term
        emb[level] = total

    def back_through(g):
        total = None
        for xx in range(4):
            term = dot(g[:, 256 * xx:256 * xx + 256], weight(0, xx))
            total = term if total is None else total + term
        return total

    gpre[...] = back_through(cot_ref[1])

    def mean_of(value):
        return jnp.mean(value, axis=-1, keepdims=True)

    summed1 = mixed[...] + emb[0]
    r1 = lax.rsqrt(mean_of(summed1 * summed1) + EPS)
    normed1 = (summed1 * r1).astype(BF16)
    mixed[...] = summed1
    proj1 = jnp.concatenate([dot_nt(normed1, weight(0, xx)) for xx in range(4)], axis=1)
    sig = jax.nn.sigmoid(proj1)
    summed2 = summed1 + proj1 * sig + emb[1]
    r2 = lax.rsqrt(mean_of(summed2 * summed2) + EPS)
    g2 = gpre[...]
    gsum = r2 * g2 - summed2 * (r2 * r2 * r2 * mean_of(g2 * summed2))
    emb[0] = gsum
    gproj = cot_ref[0].astype(F32) + gsum * (sig * (1.0 + proj1 * (1.0 - sig)))
    g1 = back_through(gproj.astype(BF16))
    summed1 = mixed[...]
    grad = emb[0] + r1 * g1 - summed1 * (r1 * r1 * r1 * mean_of(g1 * summed1))
    gb[x, yh] = grad.astype(BF16).reshape(2, 32, 1024)

    cal, cbe = pl.ds(0, 512), pl.ds(512, 512)

    def same(win, device):
        return go.send(win, win, device)

    def pieces(*idx):
        return gb.at[idx]

    bx1_p = go.send(pieces(x, yh, 0, slice(None), cbe), grb.at[0], yp)
    bx1_m = go.send(pieces(x, yh, 1, slice(None), cbe), grb.at[1], ym)
    own_a = gb.at[x, yh, :, :, cal]
    ax_p, ax_m = same(own_a, xp), same(own_a, xm)
    bx1_p.wait_recv()
    bx1_m.wait_recv()
    b2_p = go.send(grb.at[0], gb.at[x, at_y(-1) // 2, 0, :, cbe], yp)
    b2_m = go.send(grb.at[1], gb.at[x, at_y(1) // 2, 1, :, cbe], ym)
    ax_p.wait_recv()
    ax_m.wait_recv()
    ax2_p = same(gb.at[at_x(-1), yh, 0, :, cal], xp)
    ax2_m = same(gb.at[at_x(1), yh, 1, :, cal], xm)
    b2_p.wait_recv()
    b2_m.wait_recv()
    own_b = gb.at[x, :, :, :, cbe]
    bx_p, bx_m = same(own_b, xp), same(own_b, xm)
    ax2_p.wait_recv()
    ax2_m.wait_recv()
    ay_p = go.send(gb.at[:, yh, 0, :, cal], gra.at[0], yp)
    ay_m = go.send(gb.at[:, yh, 1, :, cal], gra.at[1], ym)
    bx_p.wait_recv()
    bx_m.wait_recv()
    bx2_p = same(gb.at[at_x(-1), 0, :, :, cbe], xp)
    bx2_m = same(gb.at[at_x(1), 1, :, :, cbe], xm)
    ay_p.wait_recv()
    ay_m.wait_recv()
    af_p = go.send(gra.at[0], gb.at[:, at_y(-1) // 2, 0, :, cal], yp)
    af_m = go.send(gra.at[1], gb.at[:, at_y(1) // 2, 1, :, cal], ym)

    def weight_grad(j):
        block = gb[:, :, :, :, 256 * j:256 * j + 256].reshape(512, 256)
        wg[4 * j:4 * j + 4] = dot_tn(block, att[...]).astype(BF16).reshape(4, 2, 32, 512)

    bx2_p.wait_recv()
    bx2_m.wait_recv()
    weight_grad(2)
    weight_grad(3)
    wg_b = go.send(wg.at[pl.ds(8, 8), 1 - c], wgr.at[pl.ds(8, 8)], mate)
    af_p.wait_recv()
    af_m.wait_recv()
    weight_grad(0)
    weight_grad(1)
    wg_a = go.send(wg.at[pl.ds(0, 8), 1 - c], wgr.at[pl.ds(0, 8)], mate)

    for j in range(2):
        total = None
        for zz in range(4):
            term = dot(
                gb[:, :, :, :, 256 * zz:256 * zz + 256].reshape(512, 256),
                proj[4 * zz:4 * zz + 4, :, :, 256 * j:256 * j + 256].reshape(256, 256),
            )
            total = term if total is None else total + term
        ga[:, 256 * j:256 * j + 256] = total.astype(BF16)

    for i in range(4):
        b_own[i] = dot_tn(q_ref[:, hs(i)], ga[:, hs(i)]).astype(BF16)
    back_copy = go.send(b_own, b_recv, mate)
    wg_b.wait_recv()
    wg_a.wait_recv()

    def own_chunk(j):
        return wg[j, c].astype(F32) + wgr[j].astype(F32)

    def ring_step(step, last_r, last_l):
        if step <= 7:
            value = own_chunk(at_z(8 - step))
            if last_r is not None:
                last_r.wait_recv()
                value = value + zrecv_r[step - 2].astype(F32)
            zsend_r[step - 1] = value.astype(BF16)
            last_r = go.send(zsend_r.at[step - 1], zrecv_r.at[step - 1], zp)
        value = own_chunk(at_z(step - 9))
        if last_l is not None:
            last_l.wait_recv()
            value = value + zrecv_l[step - 2].astype(F32)
        zsend_l[step - 1] = value.astype(BF16)
        last_l = go.send(zsend_l.at[step - 1], zrecv_l.at[step - 1], zm)
        return last_r, last_l

    def backward(i):
        q0_, q1_ = q_ref[top, hs(i)], q_ref[bot, hs(i)]
        k0_, k1_ = k_ref[top, hs(i)], k_ref[bot, hs(i)]
        v0_, v1_ = v_ref[top, hs(i)], v_ref[bot, hs(i)]
        a0_, a1_ = ga[top, hs(i)], ga[bot, hs(i)]
        m00, m10, m11 = scores_of(ga, v_ref, i)
        e, b = s_in[i], b_in[i]
        gq_ref[top, hs(i)] = (scale * (dot(m00, k0_) + dot_nt(a0_, e))).astype(BF16)
        gq_ref[bot, hs(i)] = (
            scale * (dot(m10, k0_) + dot(m11, k1_) + dot_nt(a1_, e))
        ).astype(BF16)
        gk_ref[top, hs(i)] = (
            scale * (dot_tn(m00, q0_) + dot_tn(m10, q1_) + dot_nt(v0_, b))
        ).astype(BF16)
        gk_ref[bot, hs(i)] = (scale * (dot_tn(m11, q1_) + dot_nt(v1_, b))).astype(BF16)
        gv_ref[top, hs(i)] = (
            scale * (dot_tn(sc[i, 0], a0_) + dot_tn(sc[i, 1], a1_) + dot(k0_, b))
        ).astype(BF16)
        gv_ref[bot, hs(i)] = (scale * (dot_tn(sc[i, 2], a1_) + dot(k1_, b))).astype(BF16)

    last_r, last_l = ring_step(1, None, None)
    back_copy.wait_recv()
    bt_own[...] = (b_own[...].astype(F32) + b_recv[...].astype(F32)).astype(BF16)
    back_pair = go.send(bt_own, bt_recv, pair)
    for step in range(2, 9):
        last_r, last_l = ring_step(step, last_r if step <= 7 else last_r, last_l)
        if step == 3:
            back_pair.wait_recv()
            b_in[...] = (
                (1.0 - cf) * b_recv[...].astype(F32) + (1.0 - ylf) * bt_recv[...].astype(F32)
            ).astype(BF16)
        if 3 <= step <= 6:
            backward(step - 3)
    last_r.wait_recv()
    last_l.wait_recv()
    y_own[...] = (
        own_chunk(z) + zrecv_r[6].astype(F32) + zrecv_l[7].astype(F32)
    ).astype(BF16)
    y_copy = go.send(y_own, y_recv, pair)
    y_copy.wait_recv()
    o_own[...] = y_own[...].astype(F32) + y_recv[...].astype(F32)
    o_copy = go.send(o_own, o_recv, mate)
    go_ref[pl.ds(pl.multiple_of(mine, 32), 32), :] = o_own[...]
    o_copy.wait_recv()
    go_ref[pl.ds(pl.multiple_of(32 - mine, 32), 32), :] = o_recv[...]
    go.drain()


def on_device(queries, keys, values, out_proj, depth_proj, code_table, code_ids, depth_cotangent):
    scale = 2048.0 ** (-0.5)
    stacked = jnp.concatenate([depth_proj.T[None], code_table], axis=0)
    packed = (
        stacked.reshape(3, 8, 4, 2, 128).transpose(2, 0, 3, 1, 4).reshape(4, 3, 16, 128)
    )
    cot = jnp.transpose(depth_cotangent[0], (1, 0, 2))

    def vm(shape, kind=BF16):
        return pltpu.VMEM(shape, kind)

    state = vm((4, DH, DH))
    gq, gk, gv, gop = pl.pallas_call(
        functools.partial(kernel, scale),
        out_shape=(
            jax.ShapeDtypeStruct((512, 512), BF16),
            jax.ShapeDtypeStruct((512, 512), BF16),
            jax.ShapeDtypeStruct((512, 512), BF16),
            jax.ShapeDtypeStruct((64, 512), F32),
        ),
        in_specs=[pl.BlockSpec(memory_space=pltpu.VMEM)] * 7,
        out_specs=(pl.BlockSpec(memory_space=pltpu.VMEM),) * 4,
        scratch_shapes=[
            vm((16, 3, 16, 128)), vm((16, 2, 32, 512)), vm((3, 4, 2, 2, 64, 1024)),
            state, state, state, state, state,
            state, state, state, state, state,
            vm((4, 3, 256, 256)), vm((512, 512), F32), vm((512, 512)),
            vm((4, 2, 2, 32, 1024)),
            vm((2, 32, 512)), vm((2, 32, 512)),
            vm((2, 2, 32, 512)), vm((2, 2, 32, 512)),
            vm((2, 32, 512)), vm((2, 32, 512)), vm((2, 32, 512)),
            vm((2, 4, 32, 512)), vm((2, 4, 32, 512)),
            vm((4, 2, 32, 512)), vm((2, 32, 512)), vm((2, 2, 32, 512)),
            vm((64, 1024), F32), vm((2, 64, 1024), F32), vm((64, 1024), F32),
            vm((4, 2, 2, 32, 1024)), vm((2, 4, 32, 512)), vm((2, 32, 512)),
            vm((512, 512)), vm((16, 2, 32, 512)), vm((16, 32, 512)),
            vm((7, 32, 512)), vm((7, 32, 512)), vm((8, 32, 512)), vm((8, 32, 512)),
            vm((32, 512)), vm((32, 512)), vm((32, 512), F32), vm((32, 512), F32),
            pltpu.SemaphoreType.DMA((N_COPIES,)),
            pltpu.SemaphoreType.DMA((N_COPIES,)),
        ],
        compiler_params=pltpu.CompilerParams(
            collective_id=0, has_side_effects=True, vmem_limit_bytes=60 * 1024 * 1024
        ),
        name="fused_step",
    )(
        queries[0], keys[0], values[0], out_proj.T, packed, code_ids[0], cot,
    )
    return gq[None], gk[None], gv[None], gop.T


def solution(mesh):
    in_specs = (
        P("dp", "seq", "head"),
        P("dp", "seq", "head"),
        P("dp", "seq", "head"),
        P("head", "dp"),
        P(None, ("head", "dp")),
        P(None, ("head", "dp"), None),
        P("dp", ("seq", "head"), None),
        P("dp", ("seq", "head"), None, None),
    )
    out_specs = (
        P("dp", "seq", "head"),
        P("dp", "seq", "head"),
        P("dp", "seq", "head"),
        P("head", "dp"),
    )
    return jax.shard_map(
        on_device, mesh=mesh, in_specs=in_specs, out_specs=out_specs, check_vma=False
    )
```

```python
import functools

import jax
import jax.numpy as jnp
from jax import lax
from jax.experimental import pallas as pl
from jax.experimental.pallas import tpu as pltpu
from jax.sharding import PartitionSpec as P

DH = 128
F32 = jnp.float32
BF16 = jnp.bfloat16
EPS = 1e-05
HALF = 256
N_COPIES = 256


def dot(a, b):
    return lax.dot_general(a, b, (((1,), (0,)), ((), ())), preferred_element_type=F32)


def dot_nt(a, b):
    return lax.dot_general(a, b, (((1,), (1,)), ((), ())), preferred_element_type=F32)


def dot_tn(a, b):
    return lax.dot_general(a, b, (((0,), (0,)), ((), ())), preferred_element_type=F32)


class Copies:
    def __init__(self, send_sems, recv_sems):
        self.send_sems, self.recv_sems, self.all = send_sems, recv_sems, []

    def send(self, src, dst, device):
        index = len(self.all)
        copy = pltpu.make_async_remote_copy(
            src_ref=src,
            dst_ref=dst,
            send_sem=self.send_sems.at[index],
            recv_sem=self.recv_sems.at[index],
            device_id=device,
            device_id_type=pl.DeviceIdType.MESH,
        )
        copy.start()
        self.all.append(copy)
        return copy

    def drain(self):
        for copy in self.all:
            copy.wait_send()


def kernel(
    scale,
    q_ref, k_ref, v_ref, op_ref, dp_ref, tab_ref, ids_ref, cot_ref,
    gq_ref, gk_ref, gv_ref, go_ref,
    wz, proj, wts,
    s_own, s_recv, t_own, t_recv, s_in,
    b_own, b_recv, bt_own, bt_recv, b_in,
    sc, acc, att,
    mix, ra1, rb1, ra2, rb2, ray, rar, raf, rbr, rbf, yb, sb1, sb2,
    mixed, emb, gpre,
    gb, gra, grb,
    ga, wg, wgr, zsend, zrecv, y_own, y_recv, o_own, o_recv,
    send_sems, recv_sems,
):
    seq, head, z = lax.axis_index("seq"), lax.axis_index("head"), lax.axis_index("dp")
    x, yh, yl, c = head // 2, head % 2, seq // 2, seq % 2
    y = 2 * yh + yl
    nz = 16

    def at_x(step):
        return (x + step + 4) % 4

    def at_y(step):
        return (y + step + 4) % 4

    def at_z(step):
        return (z + step + nz) % nz

    def dev(x_=None, y_=None, z_=None, c_=None):
        x_ = x if x_ is None else x_
        y_ = y if y_ is None else y_
        z_ = z if z_ is None else z_
        c_ = c if c_ is None else c_
        return {"seq": 2 * (y_ % 2) + c_, "head": 2 * x_ + y_ // 2, "dp": z_}

    xp, xm = dev(x_=at_x(1)), dev(x_=at_x(-1))
    yp, ym = dev(y_=at_y(1)), dev(y_=at_y(-1))
    zp, zm = dev(z_=at_z(1)), dev(z_=at_z(-1))
    zp2, zm2 = dev(z_=at_z(2)), dev(z_=at_z(-2))
    mate = dev(c_=1 - c)
    pair = dev(y_=2 * yh + 1 - yl)
    cf, ylf = c.astype(F32), yl.astype(F32)
    go = Copies(send_sems, recv_sems)

    barrier = pltpu.get_barrier_semaphore()
    for other in (xp, xm, yp, ym, zp, zm, zp2, zm2, mate):
        pl.semaphore_signal(barrier, inc=1, device_id=other, device_id_type=pl.DeviceIdType.MESH)

    def hs(i):
        return slice(i * DH, (i + 1) * DH)

    quarter = 2 * c + yl
    mine = c * 32
    qown = pl.ds(pl.multiple_of(quarter * 256, 256), 256)
    for a in range(3):
        rows8 = (dp_ref[:, qown] if a == 0 else tab_ref[a - 1, :, qown]).astype(F32)
        wz[3, a] = jnp.concatenate([rows8[:, :128], rows8[:, 128:]], axis=0).astype(BF16)
    for i in range(4):
        s_own[i] = dot_tn(k_ref[:, hs(i)], v_ref[:, hs(i)]).astype(BF16)
    pl.semaphore_wait(barrier, 9)

    state_copy = go.send(s_own, s_recv, mate)
    own_p = op_ref.at[pl.ds(pl.multiple_of(mine, 32), 32), :]

    w_came, p_came, to_mate = {}, {}, []

    def slot(rel):
        return (rel + 3) % nz

    def send_wz(rel, hop, device):
        w_came[rel - hop] = go.send(wz.at[slot(rel)], wz.at[slot(rel - hop)], device)

    def send_p(rel, hop, device):
        window = proj.at[at_z(rel), c]
        p_came[rel - hop] = go.send(own_p if rel == 0 else window, window, device)

    def p_wait(rel):
        p_came[rel].wait_recv()
        window = proj.at[at_z(rel), c]
        to_mate.append(go.send(window, window, mate))

    around = ((1, zp), (-1, zm), (2, zp2), (-2, zm2))
    for hop, device in around:
        send_wz(0, hop, device)
    for hop, device in around:
        send_p(0, hop, device)
    proj[z] = op_ref[...].reshape(2, 32, 512)

    def relay_w(j):
        for sign, device in ((-1, zp2), (1, zm2)):
            for rel in (sign * (2 * j - 1), sign * 2 * j):
                w_came[rel].wait_recv()
                if rel != 6:
                    send_wz(rel, -2 * sign, device)

    def relay_p(j):
        for sign, device in ((-1, zp2), (1, zm2)):
            for rel in (sign * (2 * j - 1), sign * 2 * j):
                p_came[rel].wait_recv()
                if rel != 6:
                    send_p(rel, -2 * sign, device)
        for sign in (-1, 1):
            for rel in (sign * (2 * j - 1), sign * 2 * j):
                window = proj.at[at_z(rel), c]
                to_mate.append(go.send(window, window, mate))

    rows = lax.broadcasted_iota(jnp.int32, (HALF, HALF), 0)
    cols = lax.broadcasted_iota(jnp.int32, (HALF, HALF), 1)
    low = rows >= cols
    top, bot = slice(0, HALF), slice(HALF, 2 * HALF)

    def scores_of(a_ref, b_ref, i):
        a0, a1 = a_ref[top, hs(i)], a_ref[bot, hs(i)]
        b0, b1 = b_ref[top, hs(i)], b_ref[bot, hs(i)]
        m00 = jnp.where(low, dot_nt(a0, b0), 0.0).astype(BF16)
        m10 = dot_nt(a1, b0).astype(BF16)
        m11 = jnp.where(low, dot_nt(a1, b1), 0.0).astype(BF16)
        return m00, m10, m11

    def forward(i):
        m00, m10, m11 = scores_of(q_ref, k_ref, i)
        sc[i, 0], sc[i, 1], sc[i, 2] = m00, m10, m11
        v0, v1 = v_ref[top, hs(i)], v_ref[bot, hs(i)]
        acc[top, hs(i)] = dot(m00, v0)
        acc[bot, hs(i)] = dot(m10, v0) + dot(m11, v1)

    def pass_state():
        state_copy.wait_recv()
        t_own[...] = (s_own[...].astype(F32) + s_recv[...].astype(F32)).astype(BF16)
        return go.send(t_own, t_recv, pair)

    def finish_attended():
        pair_copy.wait_recv()
        s_in[...] = (cf * s_recv[...].astype(F32) + ylf * t_recv[...].astype(F32)).astype(BF16)
        for i in range(4):
            att[:, hs(i)] = (
                scale * (acc[:, hs(i)] + dot(q_ref[:, hs(i)], s_in[i]))
            ).astype(BF16)

    q0 = pl.multiple_of(quarter * 256, 256)
    ccols = pl.ds(pl.multiple_of(c * 512, 512), 512)

    def qcols(y_):
        return pl.ds(pl.multiple_of((2 * c + y_ % 2) * 256, 256), 256)

    def same(win, device):
        return go.send(win, win, device)

    w_mate = []

    class Plane:
        def __init__(self, group):
            self.g = group
            for a in range(3):
                block = wz[group * 8:group * 8 + 8, a].astype(F32)
                piece = jnp.concatenate(
                    [block[:, :8].reshape(64, 128), block[:, 8:].reshape(64, 128)], axis=1
                )
                wts[a, x, yh, group, :, pl.ds(q0, 256)] = piece.astype(BF16)
            self.wait_for = (
                same(self.ax(x, 0, 32), xp), same(self.ax(x, 0, 32), xm),
                same(self.by(y, 32, 32), yp), same(self.by(y, 32, 32), ym),
            )

        def ax(self, xx, r0, n):
            return wts.at[:, xx, yh, self.g, pl.ds(r0, n), qcols(y)]

        def by(self, yy, r0, n):
            return wts.at[:, x, yy // 2, self.g, pl.ds(r0, n), qcols(yy)]

        def ay(self, yy, r0, n):
            return wts.at[:, :, yy // 2, self.g, pl.ds(r0, n), qcols(yy)]

        def bx(self, xx, r0, n):
            return wts.at[:, xx, :, self.g, pl.ds(r0, n), ccols]

        def arrived(self):
            for copy in self.wait_for:
                copy.wait_recv()

        def second(self):
            self.arrived()
            self.wait_for = (
                same(self.ax(at_x(-1), 0, 16), xp), same(self.ax(at_x(1), 16, 16), xm),
                same(self.by(at_y(-1), 32, 16), yp), same(self.by(at_y(1), 48, 16), ym),
            )

        def third(self):
            self.arrived()
            self.wait_for = (
                same(self.ay(y, 0, 32), yp), same(self.ay(y, 0, 32), ym),
                same(self.bx(x, 32, 32), xp), same(self.bx(x, 32, 32), xm),
            )
            w_mate.append(same(self.ay(y, 0, 32), mate))
            w_mate.append(same(self.bx(x, 32, 32), mate))

        def fourth(self):
            self.arrived()
            self.wait_for = (
                same(self.ay(at_y(-1), 0, 16), yp), same(self.ay(at_y(1), 16, 16), ym),
                same(self.bx(at_x(-1), 32, 16), xp), same(self.bx(at_x(1), 48, 16), xm),
            )
            for step in (-1, 1):
                w_mate.append(same(self.ay(at_y(step), 0, 32), mate))
                w_mate.append(same(self.bx(at_x(step), 32, 32), mate))

        def fifth(self):
            self.arrived()
            w_mate.append(same(self.ay(at_y(2), 0, 32), mate))
            w_mate.append(same(self.bx(at_x(2), 32, 32), mate))

    forward(0)
    pair_copy = pass_state()
    forward(1)
    relay_w(1)
    relay_p(1)
    forward(2)
    forward(3)
    relay_w(2)
    near = Plane(0)
    relay_p(2)
    finish_attended()
    relay_w(3)
    near.second()
    relay_p(3)
    for rel in (-7, -8, 7):
        w_came[rel].wait_recv()
    far = Plane(1)
    near.third()
    for rel in (-7, -8, 7):
        p_wait(rel)
    for copy in to_mate:
        copy.wait_recv()

    def mix_block(j):
        part = dot_nt(att[...], proj[4 * j:4 * j + 4].reshape(256, 512))
        mix[:, :, :, :, 256 * j:256 * j + 256] = part.astype(BF16).reshape(4, 2, 2, 32, 256)

    al, be = slice(0, 512), slice(512, 1024)
    mix_block(2)
    mix_block(3)
    mby_p = go.send(mix.at[:, 1 - yh, 0, :, pl.ds(512, 512)], rbr.at[0], yp)
    mby_m = go.send(mix.at[:, 1 - yh, 1, :, pl.ds(512, 512)], rbr.at[1], ym)
    mix_block(0)
    mix_block(1)
    max_p = go.send(mix.at[at_x(2), 0, :, :, pl.ds(0, 512)], ra1, xp)
    max_m = go.send(mix.at[at_x(2), 1, :, :, pl.ds(0, 512)], rb1, xm)

    far.second()

    mby_p.wait_recv()
    mby_m.wait_recv()
    mbf_p = go.send(rbr.at[0], rbf.at[0], yp)
    mbf_m = go.send(rbr.at[1], rbf.at[1], ym)
    max_p.wait_recv()
    max_m.wait_recv()
    mix[at_x(1), 0, :, :, al] = (
        mix[at_x(1), 0, :, :, al].astype(F32) + ra1[...].astype(F32)
    ).astype(BF16)
    mix[at_x(-1), 1, :, :, al] = (
        mix[at_x(-1), 1, :, :, al].astype(F32) + rb1[...].astype(F32)
    ).astype(BF16)
    max2_p = go.send(mix.at[at_x(1), :, :, :, pl.ds(0, 512)], ra2, xp)
    max2_m = go.send(mix.at[at_x(-1), :, :, :, pl.ds(0, 512)], rb2, xm)

    near.fourth()
    far.third()
    mbf_p.wait_recv()
    mbf_m.wait_recv()
    for hf in range(2):
        yb[:, hf] = (
            mix[:, yh, hf, :, be].astype(F32) + rbf[hf].astype(F32)
        ).astype(BF16)
    mbx_p = go.send(yb.at[at_x(2), 0], sb1.at[0], xp)
    mbx_m = go.send(yb.at[at_x(2), 1], sb1.at[1], xm)
    max2_p.wait_recv()
    max2_m.wait_recv()
    ray[...] = (
        mix[x, 1 - yh, :, :, al].astype(F32)
        + ra2[1 - yh].astype(F32)
        + rb2[1 - yh].astype(F32)
    ).astype(BF16)
    may_p = go.send(ray.at[0], rar.at[0], yp)
    may_m = go.send(ray.at[1], rar.at[1], ym)
    mixed[:, al] = (
        mix[x, yh, :, :, al].astype(F32) + ra2[yh].astype(F32) + rb2[yh].astype(F32)
    ).reshape(64, 512)
    near.fifth()
    mbx_p.wait_recv()
    mbx_m.wait_recv()
    yb[at_x(1), 0] = (yb[at_x(1), 0].astype(F32) + sb1[0].astype(F32)).astype(BF16)
    yb[at_x(-1), 1] = (yb[at_x(-1), 1].astype(F32) + sb1[1].astype(F32)).astype(BF16)
    mbx2_p = go.send(yb.at[at_x(1)], sb2.at[0], xp)
    mbx2_m = go.send(yb.at[at_x(-1)], sb2.at[1], xm)
    may_p.wait_recv()
    may_m.wait_recv()
    maf_p = go.send(rar.at[0], raf.at[0], yp)
    maf_m = go.send(rar.at[1], raf.at[1], ym)
    far.fourth()
    maf_p.wait_recv()
    maf_m.wait_recv()
    mixed[:, al] = mixed[:, al] + raf[...].astype(F32).reshape(64, 512)
    mbx2_p.wait_recv()
    mbx2_m.wait_recv()
    mixed[:, be] = (
        yb[x].astype(F32) + sb2[0].astype(F32) + sb2[1].astype(F32)
    ).reshape(64, 512)
    far.fifth()
    for copy in w_mate:
        copy.wait_recv()

    def weight(a, xx):
        return wts[a, xx].reshape(256, 1024)

    turn = (z * 8 + 128 - 24) % 128
    place = lax.broadcasted_iota(jnp.int32, (256, 64), 0)
    vocab = place - place % 128 + (place % 128 + turn) % 128
    for level in range(2):
        ids = ids_ref[level:level + 1, :]
        total = None
        for xx in range(4):
            onehot = jnp.where(ids - 256 * xx == vocab, 1.0, 0.0).astype(BF16)
            term = dot_tn(onehot, weight(1 + level, xx))
            total = term if total is None else total + term
        emb[level] = total

    def turned(value, by):
        return jnp.concatenate(
            [pltpu.roll(value[:, 128 * j:128 * j + 128], by, 1) for j in range(8)], axis=1
        )

    def back_through(g):
        g = turned(g, (128 - turn) % 128).astype(BF16)
        total = None
        for xx in range(4):
            term = dot(g[:, 256 * xx:256 * xx + 256], weight(0, xx))
            total = term if total is None else total + term
        return total

    gpre[...] = back_through(cot_ref[:, 1, :].astype(F32))

    def mean_of(value):
        return jnp.mean(value, axis=-1, keepdims=True)

    summed1 = mixed[...] + emb[0]
    r1 = lax.rsqrt(mean_of(summed1 * summed1) + EPS)
    normed1 = (summed1 * r1).astype(BF16)
    mixed[...] = summed1
    proj1 = turned(
        jnp.concatenate([dot_nt(normed1, weight(0, xx)) for xx in range(4)], axis=1), turn
    )
    sig = jax.nn.sigmoid(proj1)
    summed2 = summed1 + proj1 * sig + emb[1]
    r2 = lax.rsqrt(mean_of(summed2 * summed2) + EPS)
    g2 = gpre[...]
    gsum = r2 * g2 - summed2 * (r2 * r2 * r2 * mean_of(g2 * summed2))
    emb[0] = gsum
    gproj = cot_ref[:, 0, :].astype(F32) + gsum * (sig * (1.0 + proj1 * (1.0 - sig)))
    g1 = back_through(gproj)
    summed1 = mixed[...]
    grad = emb[0] + r1 * g1 - summed1 * (r1 * r1 * r1 * mean_of(g1 * summed1))
    gb[x, yh] = grad.astype(BF16).reshape(2, 32, 1024)

    cal, cbe = pl.ds(0, 512), pl.ds(512, 512)

    def pieces(*idx):
        return gb.at[idx]

    bx1_p = go.send(pieces(x, yh, 0, slice(None), cbe), grb.at[0], yp)
    bx1_m = go.send(pieces(x, yh, 1, slice(None), cbe), grb.at[1], ym)
    own_a = gb.at[x, yh, :, :, cal]
    ax_p, ax_m = same(own_a, xp), same(own_a, xm)
    bx1_p.wait_recv()
    bx1_m.wait_recv()
    b2_p = go.send(grb.at[0], gb.at[x, at_y(-1) // 2, 0, :, cbe], yp)
    b2_m = go.send(grb.at[1], gb.at[x, at_y(1) // 2, 1, :, cbe], ym)
    ax_p.wait_recv()
    ax_m.wait_recv()
    ax2_p = same(gb.at[at_x(-1), yh, 0, :, cal], xp)
    ax2_m = same(gb.at[at_x(1), yh, 1, :, cal], xm)
    b2_p.wait_recv()
    b2_m.wait_recv()
    own_b = gb.at[x, :, :, :, cbe]
    bx_p, bx_m = same(own_b, xp), same(own_b, xm)
    ax2_p.wait_recv()
    ax2_m.wait_recv()
    ay_p = go.send(gb.at[:, yh, 0, :, cal], gra.at[0], yp)
    ay_m = go.send(gb.at[:, yh, 1, :, cal], gra.at[1], ym)
    bx_p.wait_recv()
    bx_m.wait_recv()
    bx2_p = same(gb.at[at_x(-1), 0, :, :, cbe], xp)
    bx2_m = same(gb.at[at_x(1), 1, :, :, cbe], xm)
    ay_p.wait_recv()
    ay_m.wait_recv()
    af_p = go.send(gra.at[0], gb.at[:, at_y(-1) // 2, 0, :, cal], yp)
    af_m = go.send(gra.at[1], gb.at[:, at_y(1) // 2, 1, :, cal], ym)

    def weight_grad(j):
        block = gb[:, :, :, :, 256 * j:256 * j + 256].reshape(512, 256)
        wg[4 * j:4 * j + 4] = dot_tn(block, att[...]).astype(BF16).reshape(4, 2, 32, 512)

    bx2_p.wait_recv()
    bx2_m.wait_recv()
    weight_grad(2)
    weight_grad(3)
    wg_b = go.send(wg.at[pl.ds(8, 8), 1 - c], wgr.at[pl.ds(8, 8)], mate)
    af_p.wait_recv()
    af_m.wait_recv()
    weight_grad(0)
    weight_grad(1)
    wg_a = go.send(wg.at[pl.ds(0, 8), 1 - c], wgr.at[pl.ds(0, 8)], mate)

    for j in range(2):
        total = None
        for zz in range(4):
            term = dot(
                gb[:, :, :, :, 256 * zz:256 * zz + 256].reshape(512, 256),
                proj[4 * zz:4 * zz + 4, :, :, 256 * j:256 * j + 256].reshape(256, 256),
            )
            total = term if total is None else total + term
        ga[:, 256 * j:256 * j + 256] = total.astype(BF16)

    for i in range(4):
        b_own[i] = dot_tn(q_ref[:, hs(i)], ga[:, hs(i)]).astype(BF16)
    back_copy = go.send(b_own, b_recv, mate)
    wg_b.wait_recv()
    wg_a.wait_recv()

    def own_chunk(j):
        return wg[j, c].astype(F32) + wgr[j].astype(F32)

    chains = ((8, 4), (7, 4), (-7, 4), (-6, 3))
    came = [None] * 4

    def chain_step(m):
        for n, (first, length) in enumerate(chains):
            if m >= length:
                continue
            sign = 1 if first > 0 else -1
            dist = first - 2 * sign * m
            value = own_chunk(at_z(dist))
            if m > 0:
                came[n].wait_recv()
                value = value + zrecv[n, m - 1].astype(F32)
            zsend[n, m] = value.astype(BF16)
            device = {2: zp2, 1: zp, -1: zm, -2: zm2}[max(-2, min(2, dist))]
            came[n] = go.send(zsend.at[n, m], zrecv.at[n, m], device)

    def backward(i):
        q0_, q1_ = q_ref[top, hs(i)], q_ref[bot, hs(i)]
        k0_, k1_ = k_ref[top, hs(i)], k_ref[bot, hs(i)]
        v0_, v1_ = v_ref[top, hs(i)], v_ref[bot, hs(i)]
        a0_, a1_ = ga[top, hs(i)], ga[bot, hs(i)]
        m00, m10, m11 = scores_of(ga, v_ref, i)
        e, b = s_in[i], b_in[i]
        gq_ref[top, hs(i)] = (scale * (dot(m00, k0_) + dot_nt(a0_, e))).astype(BF16)
        gq_ref[bot, hs(i)] = (
            scale * (dot(m10, k0_) + dot(m11, k1_) + dot_nt(a1_, e))
        ).astype(BF16)
        gk_ref[top, hs(i)] = (
            scale * (dot_tn(m00, q0_) + dot_tn(m10, q1_) + dot_nt(v0_, b))
        ).astype(BF16)
        gk_ref[bot, hs(i)] = (scale * (dot_tn(m11, q1_) + dot_nt(v1_, b))).astype(BF16)
        gv_ref[top, hs(i)] = (
            scale * (dot_tn(sc[i, 0], a0_) + dot_tn(sc[i, 1], a1_) + dot(k0_, b))
        ).astype(BF16)
        gv_ref[bot, hs(i)] = (scale * (dot_tn(sc[i, 2], a1_) + dot(k1_, b))).astype(BF16)

    chain_step(0)
    back_copy.wait_recv()
    bt_own[...] = (b_own[...].astype(F32) + b_recv[...].astype(F32)).astype(BF16)
    back_pair = go.send(bt_own, bt_recv, pair)
    chain_step(1)
    back_pair.wait_recv()
    b_in[...] = (
        (1.0 - cf) * b_recv[...].astype(F32) + (1.0 - ylf) * bt_recv[...].astype(F32)
    ).astype(BF16)
    backward(0)
    backward(1)
    chain_step(2)
    backward(2)
    chain_step(3)
    backward(3)
    total = own_chunk(z)
    for n, (first, length) in enumerate(chains):
        came[n].wait_recv()
        total = total + zrecv[n, length - 1].astype(F32)
    y_own[...] = total.astype(BF16)
    y_copy = go.send(y_own, y_recv, pair)
    y_copy.wait_recv()
    o_own[...] = y_own[...].astype(F32) + y_recv[...].astype(F32)
    o_copy = go.send(o_own, o_recv, mate)
    go_ref[pl.ds(pl.multiple_of(mine, 32), 32), :] = o_own[...]
    o_copy.wait_recv()
    go_ref[pl.ds(pl.multiple_of(32 - mine, 32), 32), :] = o_recv[...]
    go.drain()


def on_device(queries, keys, values, out_proj, depth_proj, code_table, code_ids, depth_cotangent):
    scale = 2048.0 ** (-0.5)
    def vm(shape, kind=BF16):
        return pltpu.VMEM(shape, kind)

    state = vm((4, DH, DH))
    gq, gk, gv, gop = pl.pallas_call(
        functools.partial(kernel, scale),
        out_shape=(
            jax.ShapeDtypeStruct((512, 512), BF16),
            jax.ShapeDtypeStruct((512, 512), BF16),
            jax.ShapeDtypeStruct((512, 512), BF16),
            jax.ShapeDtypeStruct((64, 512), F32),
        ),
        in_specs=[pl.BlockSpec(memory_space=pltpu.VMEM)] * 8,
        out_specs=(pl.BlockSpec(memory_space=pltpu.VMEM),) * 4,
        scratch_shapes=[
            vm((16, 3, 16, 128)), vm((16, 2, 32, 512)), vm((3, 4, 2, 2, 64, 1024)),
            state, state, state, state, state,
            state, state, state, state, state,
            vm((4, 3, 256, 256)), vm((512, 512), F32), vm((512, 512)),
            vm((4, 2, 2, 32, 1024)),
            vm((2, 32, 512)), vm((2, 32, 512)),
            vm((2, 2, 32, 512)), vm((2, 2, 32, 512)),
            vm((2, 32, 512)), vm((2, 32, 512)), vm((2, 32, 512)),
            vm((2, 4, 32, 512)), vm((2, 4, 32, 512)),
            vm((4, 2, 32, 512)), vm((2, 32, 512)), vm((2, 2, 32, 512)),
            vm((64, 1024), F32), vm((2, 64, 1024), F32), vm((64, 1024), F32),
            vm((4, 2, 2, 32, 1024)), vm((2, 4, 32, 512)), vm((2, 32, 512)),
            vm((512, 512)), vm((16, 2, 32, 512)), vm((16, 32, 512)),
            vm((4, 4, 32, 512)), vm((4, 4, 32, 512)),
            vm((32, 512)), vm((32, 512)), vm((32, 512), F32), vm((32, 512), F32),
            pltpu.SemaphoreType.DMA((N_COPIES,)),
            pltpu.SemaphoreType.DMA((N_COPIES,)),
        ],
        compiler_params=pltpu.CompilerParams(
            collective_id=0, has_side_effects=True, vmem_limit_bytes=34 * 1024 * 1024
        ),
        name="fused_step",
    )(
        queries[0], keys[0], values[0], out_proj.T, depth_proj.T, code_table, code_ids[0].T,
        depth_cotangent[0],
    )
    return gq[None], gk[None], gv[None], gop.T


def solution(mesh):
    in_specs = (
        P("dp", "seq", "head"),
        P("dp", "seq", "head"),
        P("dp", "seq", "head"),
        P("head", "dp"),
        P(None, ("head", "dp")),
        P(None, ("head", "dp"), None),
        P("dp", ("seq", "head"), None),
        P("dp", ("seq", "head"), None, None),
    )
    out_specs = (
        P("dp", "seq", "head"),
        P("dp", "seq", "head"),
        P("dp", "seq", "head"),
        P("head", "dp"),
    )
    return jax.shard_map(
        on_device, mesh=mesh, in_specs=in_specs, out_specs=out_specs, check_vma=False
    )
```

```python
import functools

import jax
import jax.numpy as jnp
from jax import lax
from jax.experimental import pallas as pl
from jax.experimental.pallas import tpu as pltpu
from jax.sharding import PartitionSpec as P

DH = 128
F32 = jnp.float32
BF16 = jnp.bfloat16
EPS = 1e-05
HALF = 256
N_COPIES = 256


def dot(a, b):
    return lax.dot_general(a, b, (((1,), (0,)), ((), ())), preferred_element_type=F32)


def dot_nt(a, b):
    return lax.dot_general(a, b, (((1,), (1,)), ((), ())), preferred_element_type=F32)


def dot_tn(a, b):
    return lax.dot_general(a, b, (((0,), (0,)), ((), ())), preferred_element_type=F32)


class Copies:
    def __init__(self, send_sems, recv_sems):
        self.send_sems, self.recv_sems, self.all = send_sems, recv_sems, []

    def send(self, src, dst, device):
        index = len(self.all)
        copy = pltpu.make_async_remote_copy(
            src_ref=src,
            dst_ref=dst,
            send_sem=self.send_sems.at[index],
            recv_sem=self.recv_sems.at[index],
            device_id=device,
            device_id_type=pl.DeviceIdType.MESH,
        )
        copy.start()
        self.all.append(copy)
        return copy

    def drain(self):
        for copy in self.all:
            copy.wait_send()


def kernel(
    scale,
    q_in, k_in, v_in, op_in, dp_in, tab_in, ids_in, cot_in,
    gq_ref, gk_ref, gv_ref, go_ref,
    q_ref, k_ref, v_ref, op_ref, dp_ref, tab_ref, ids_ref, cot_ref, load_sems,
    wz, proj, wts,
    s_own, s_recv, t_own, t_recv, s_in,
    b_own, b_recv, bt_own, bt_recv, b_in,
    sc, acc, att,
    mix, ra1, rb1, ra2, rb2, ray, rar, raf, rbr, rbf, yb, sb1, sb2,
    mixed, emb, gpre,
    gb, gra, grb,
    ga, wg, wgr, zsend, zrecv, y_own, y_recv, o_own, o_recv,
    send_sems, recv_sems,
):
    seq, head, z = lax.axis_index("seq"), lax.axis_index("head"), lax.axis_index("dp")
    x, yh, yl, c = head // 2, head % 2, seq // 2, seq % 2
    y = 2 * yh + yl
    nz = 16

    def at_x(step):
        return (x + step + 4) % 4

    def at_y(step):
        return (y + step + 4) % 4

    def at_z(step):
        return (z + step + nz) % nz

    def dev(x_=None, y_=None, z_=None, c_=None):
        x_ = x if x_ is None else x_
        y_ = y if y_ is None else y_
        z_ = z if z_ is None else z_
        c_ = c if c_ is None else c_
        return {"seq": 2 * (y_ % 2) + c_, "head": 2 * x_ + y_ // 2, "dp": z_}

    xp, xm = dev(x_=at_x(1)), dev(x_=at_x(-1))
    yp, ym = dev(y_=at_y(1)), dev(y_=at_y(-1))
    zp, zm = dev(z_=at_z(1)), dev(z_=at_z(-1))
    zp2, zm2 = dev(z_=at_z(2)), dev(z_=at_z(-2))
    mate = dev(c_=1 - c)
    pair = dev(y_=2 * yh + 1 - yl)
    cf, ylf = c.astype(F32), yl.astype(F32)
    go = Copies(send_sems, recv_sems)

    barrier = pltpu.get_barrier_semaphore()
    for other in (xp, xm, yp, ym, zp, zm, zp2, zm2, mate):
        pl.semaphore_signal(barrier, inc=1, device_id=other, device_id_type=pl.DeviceIdType.MESH)

    def hs(i):
        return slice(i * DH, (i + 1) * DH)

    loads = [
        pltpu.make_async_copy(src, dst, load_sems.at[n])
        for n, (src, dst) in enumerate((
            (dp_in, dp_ref), (tab_in, tab_ref), (k_in, k_ref), (v_in, v_ref),
            (q_in, q_ref), (op_in, op_ref), (ids_in, ids_ref), (cot_in, cot_ref),
        ))
    ]
    for load in loads:
        load.start()
    quarter = 2 * c + yl
    loads[0].wait()
    loads[1].wait()
    mine = c * 32
    qown = pl.ds(pl.multiple_of(quarter * 256, 256), 256)
    for a in range(3):
        rows8 = (dp_ref[:, qown] if a == 0 else tab_ref[a - 1, :, qown]).astype(F32)
        wz[3, a] = jnp.concatenate([rows8[:, :128], rows8[:, 128:]], axis=0).astype(BF16)
    loads[2].wait()
    loads[3].wait()
    for i in range(4):
        s_own[i] = dot_tn(k_ref[:, hs(i)], v_ref[:, hs(i)]).astype(BF16)
    for load in loads[4:]:
        load.wait()
    pl.semaphore_wait(barrier, 9)

    state_copy = go.send(s_own, s_recv, mate)
    own_p = op_ref.at[pl.ds(pl.multiple_of(mine, 32), 32), :]

    w_came, p_came, to_mate = {}, {}, {}

    def slot(rel):
        return (rel + 3) % nz

    def send_wz(rel, hop, device):
        w_came[rel - hop] = go.send(wz.at[slot(rel)], wz.at[slot(rel - hop)], device)

    def send_p(rel, hop, device):
        src = own_p if rel == 0 else proj.at[slot(rel), c]
        p_came[rel - hop] = go.send(src, proj.at[slot(rel - hop), c], device)

    def p_mate(rel):
        window = proj.at[slot(rel), c]
        to_mate[rel] = go.send(window, window, mate)

    around = ((1, zp), (-1, zm), (2, zp2), (-2, zm2))
    for hop, device in around:
        send_wz(0, hop, device)
    for hop, device in around:
        send_p(0, hop, device)
    proj[3] = op_ref[...].reshape(2, 32, 512)

    def relay_w(j):
        for sign, device in ((-1, zp2), (1, zm2)):
            for rel in (sign * (2 * j - 1), sign * 2 * j):
                w_came[rel].wait_recv()
                if rel != 6:
                    send_wz(rel, -2 * sign, device)

    def relay_p(j):
        for sign, device in ((-1, zp2), (1, zm2)):
            for rel in (sign * (2 * j - 1), sign * 2 * j):
                p_came[rel].wait_recv()
                if rel != 6:
                    send_p(rel, -2 * sign, device)
        for sign in (-1, 1):
            for rel in (sign * (2 * j - 1), sign * 2 * j):
                p_mate(rel)

    rows = lax.broadcasted_iota(jnp.int32, (HALF, HALF), 0)
    cols = lax.broadcasted_iota(jnp.int32, (HALF, HALF), 1)
    low = rows >= cols
    top, bot = slice(0, HALF), slice(HALF, 2 * HALF)

    def scores_of(a_ref, b_ref, i):
        a0, a1 = a_ref[top, hs(i)], a_ref[bot, hs(i)]
        b0, b1 = b_ref[top, hs(i)], b_ref[bot, hs(i)]
        m00 = jnp.where(low, dot_nt(a0, b0), 0.0).astype(BF16)
        m10 = dot_nt(a1, b0).astype(BF16)
        m11 = jnp.where(low, dot_nt(a1, b1), 0.0).astype(BF16)
        return m00, m10, m11

    def forward(i):
        m00, m10, m11 = scores_of(q_ref, k_ref, i)
        sc[i, 0], sc[i, 1], sc[i, 2] = m00, m10, m11
        v0, v1 = v_ref[top, hs(i)], v_ref[bot, hs(i)]
        acc[top, hs(i)] = dot(m00, v0)
        acc[bot, hs(i)] = dot(m10, v0) + dot(m11, v1)

    def pass_state():
        state_copy.wait_recv()
        t_own[...] = (s_own[...].astype(F32) + s_recv[...].astype(F32)).astype(BF16)
        return go.send(t_own, t_recv, pair)

    def finish_attended():
        pair_copy.wait_recv()
        s_in[...] = (cf * s_recv[...].astype(F32) + ylf * t_recv[...].astype(F32)).astype(BF16)
        for i in range(4):
            att[:, hs(i)] = (
                scale * (acc[:, hs(i)] + dot(q_ref[:, hs(i)], s_in[i]))
            ).astype(BF16)

    q0 = pl.multiple_of(quarter * 256, 256)
    ccols = pl.ds(pl.multiple_of(c * 512, 512), 512)

    def qcols(y_):
        return pl.ds(pl.multiple_of((2 * c + y_ % 2) * 256, 256), 256)

    def same(win, device):
        return go.send(win, win, device)

    w_mate = []

    class Plane:
        def __init__(self, group):
            self.g = group
            for a in range(3):
                block = wz[group * 8:group * 8 + 8, a].astype(F32)
                piece = jnp.concatenate(
                    [block[:, :8].reshape(64, 128), block[:, 8:].reshape(64, 128)], axis=1
                )
                wts[a, x, yh, group, :, pl.ds(q0, 256)] = piece.astype(BF16)
            self.wait_for = (
                same(self.ax(x, 0, 32), xp), same(self.ax(x, 0, 32), xm),
                same(self.by(y, 32, 32), yp), same(self.by(y, 32, 32), ym),
            )

        def ax(self, xx, r0, n):
            return wts.at[:, xx, yh, self.g, pl.ds(r0, n), qcols(y)]

        def by(self, yy, r0, n):
            return wts.at[:, x, yy // 2, self.g, pl.ds(r0, n), qcols(yy)]

        def ay(self, yy, r0, n):
            return wts.at[:, :, yy // 2, self.g, pl.ds(r0, n), qcols(yy)]

        def bx(self, xx, r0, n):
            return wts.at[:, xx, :, self.g, pl.ds(r0, n), ccols]

        def arrived(self):
            for copy in self.wait_for:
                copy.wait_recv()

        def second(self):
            self.arrived()
            self.wait_for = (
                same(self.ax(at_x(-1), 0, 16), xp), same(self.ax(at_x(1), 16, 16), xm),
                same(self.by(at_y(-1), 32, 16), yp), same(self.by(at_y(1), 48, 16), ym),
            )

        def third(self):
            self.arrived()
            self.wait_for = (
                same(self.ay(y, 0, 32), yp), same(self.ay(y, 0, 32), ym),
                same(self.bx(x, 32, 32), xp), same(self.bx(x, 32, 32), xm),
            )
            w_mate.append(same(self.ay(y, 0, 32), mate))
            w_mate.append(same(self.bx(x, 32, 32), mate))

        def fourth(self):
            self.arrived()
            self.wait_for = (
                same(self.ay(at_y(-1), 0, 16), yp), same(self.ay(at_y(1), 16, 16), ym),
                same(self.bx(at_x(-1), 32, 16), xp), same(self.bx(at_x(1), 48, 16), xm),
            )
            for step in (-1, 1):
                w_mate.append(same(self.ay(at_y(step), 0, 32), mate))
                w_mate.append(same(self.bx(at_x(step), 32, 32), mate))

        def fifth(self):
            self.arrived()
            w_mate.append(same(self.ay(at_y(2), 0, 32), mate))
            w_mate.append(same(self.bx(at_x(2), 32, 32), mate))

    class Reduce:
        def __init__(self, group):
            self.g, self.a0, self.b0 = group, 512 * group, 512 * group + 256
            self.block(2 * group + 1)
            b = pl.ds(self.b0, 256)
            self.y1 = (
                go.send(mix.at[:, 1 - yh, 0, :, b], rbr.at[group, 0], yp),
                go.send(mix.at[:, 1 - yh, 1, :, b], rbr.at[group, 1], ym),
            )
            self.block(2 * group)
            a = pl.ds(self.a0, 256)
            self.x1 = (
                go.send(mix.at[at_x(2), 0, :, :, a], ra1.at[group], xp),
                go.send(mix.at[at_x(2), 1, :, :, a], rb1.at[group], xm),
            )

        def block(self, j):
            part = dot_nt(att[...], proj[4 * j:4 * j + 4].reshape(256, 512))
            mix[:, :, :, :, 256 * j:256 * j + 256] = part.astype(BF16).reshape(4, 2, 2, 32, 256)

        def second(self):
            g, al = self.g, slice(self.a0, self.a0 + 256)
            for copy in self.y1:
                copy.wait_recv()
            self.y2 = (
                go.send(rbr.at[g, 0], rbf.at[g, 0], yp), go.send(rbr.at[g, 1], rbf.at[g, 1], ym)
            )
            for copy in self.x1:
                copy.wait_recv()
            mix[at_x(1), 0, :, :, al] = (
                mix[at_x(1), 0, :, :, al].astype(F32) + ra1[g].astype(F32)
            ).astype(BF16)
            mix[at_x(-1), 1, :, :, al] = (
                mix[at_x(-1), 1, :, :, al].astype(F32) + rb1[g].astype(F32)
            ).astype(BF16)
            a = pl.ds(self.a0, 256)
            self.x2 = (
                go.send(mix.at[at_x(1), :, :, :, a], ra2.at[g], xp),
                go.send(mix.at[at_x(-1), :, :, :, a], rb2.at[g], xm),
            )

        def third(self):
            g, al, be = self.g, slice(self.a0, self.a0 + 256), slice(self.b0, self.b0 + 256)
            for copy in self.y2:
                copy.wait_recv()
            for hf in range(2):
                yb[g, :, hf] = (
                    mix[:, yh, hf, :, be].astype(F32) + rbf[g, hf].astype(F32)
                ).astype(BF16)
            self.bx1 = (
                go.send(yb.at[g, at_x(2), 0], sb1.at[g, 0], xp),
                go.send(yb.at[g, at_x(2), 1], sb1.at[g, 1], xm),
            )
            for copy in self.x2:
                copy.wait_recv()
            ray[g] = (
                mix[x, 1 - yh, :, :, al].astype(F32)
                + ra2[g, 1 - yh].astype(F32)
                + rb2[g, 1 - yh].astype(F32)
            ).astype(BF16)
            self.ay1 = (
                go.send(ray.at[g, 0], rar.at[g, 0], yp), go.send(ray.at[g, 1], rar.at[g, 1], ym)
            )
            mixed[:, al] = (
                mix[x, yh, :, :, al].astype(F32)
                + ra2[g, yh].astype(F32)
                + rb2[g, yh].astype(F32)
            ).reshape(64, 256)

        def fourth(self):
            g = self.g
            for copy in self.bx1:
                copy.wait_recv()
            for step, hf in ((1, 0), (-1, 1)):
                yb[g, at_x(step), hf] = (
                    yb[g, at_x(step), hf].astype(F32) + sb1[g, hf].astype(F32)
                ).astype(BF16)
            self.bx2 = (
                go.send(yb.at[g, at_x(1)], sb2.at[g, 0], xp),
                go.send(yb.at[g, at_x(-1)], sb2.at[g, 1], xm),
            )
            for copy in self.ay1:
                copy.wait_recv()
            self.ay2 = (
                go.send(rar.at[g, 0], raf.at[g, 0], yp), go.send(rar.at[g, 1], raf.at[g, 1], ym)
            )

        def fifth(self):
            g, al, be = self.g, slice(self.a0, self.a0 + 256), slice(self.b0, self.b0 + 256)
            for copy in self.ay2 + self.bx2:
                copy.wait_recv()
            mixed[:, al] = mixed[:, al] + raf[g].astype(F32).reshape(64, 256)
            mixed[:, be] = (
                yb[g, x].astype(F32) + sb2[g, 0].astype(F32) + sb2[g, 1].astype(F32)
            ).reshape(64, 256)

    forward(0)
    pair_copy = pass_state()
    forward(1)
    relay_w(1)
    relay_p(1)
    forward(2)
    forward(3)
    relay_w(2)
    near = Plane(0)
    relay_p(2)
    finish_attended()
    near.second()
    for rel in (-1, -2, 1, 2, -3, 3, 4):
        to_mate[rel].wait_recv()
    mnear = Reduce(0)
    relay_w(3)
    near.third()
    relay_p(3)
    mnear.second()
    for rel in (-7, -8, 7):
        w_came[rel].wait_recv()
    far = Plane(1)
    mnear.third()
    for rel in (-7, -8, 7):
        p_came[rel].wait_recv()
        p_mate(rel)
    for rel in (-4, -5, -6, 5, 6, -7, -8, 7):
        to_mate[rel].wait_recv()
    mfar = Reduce(1)
    far.second()
    mnear.fourth()
    near.fourth()
    mfar.second()
    far.third()
    mnear.fifth()
    mfar.third()
    near.fifth()
    mfar.fourth()
    far.fourth()
    mfar.fifth()
    far.fifth()
    for copy in w_mate:
        copy.wait_recv()

    def weight(a, xx):
        return wts[a, xx].reshape(256, 1024)

    turn = (z * 8 + 128 - 24) % 128
    place = lax.broadcasted_iota(jnp.int32, (256, 64), 0)
    vocab = place - place % 128 + (place % 128 + turn) % 128
    for level in range(2):
        ids = ids_ref[level:level + 1, :]
        total = None
        for xx in range(4):
            onehot = jnp.where(ids - 256 * xx == vocab, 1.0, 0.0).astype(BF16)
            term = dot_tn(onehot, weight(1 + level, xx))
            total = term if total is None else total + term
        emb[level] = total

    def turned(value, by):
        return jnp.concatenate(
            [pltpu.roll(value[:, 128 * j:128 * j + 128], by, 1) for j in range(8)], axis=1
        )

    def back_through(g):
        g = turned(g, (128 - turn) % 128).astype(BF16)
        total = None
        for xx in range(4):
            term = dot(g[:, 256 * xx:256 * xx + 256], weight(0, xx))
            total = term if total is None else total + term
        return total

    gpre[...] = back_through(cot_ref[:, 1, :].astype(F32))

    def mean_of(value):
        return jnp.mean(value, axis=-1, keepdims=True)

    shift = (z * 64 + 1024 - 192) % 1024
    summed1 = pltpu.roll(mixed[...], shift, 1) + emb[0]
    r1 = lax.rsqrt(mean_of(summed1 * summed1) + EPS)
    normed1 = (summed1 * r1).astype(BF16)
    mixed[...] = summed1
    proj1 = turned(
        jnp.concatenate([dot_nt(normed1, weight(0, xx)) for xx in range(4)], axis=1), turn
    )
    sig = jax.nn.sigmoid(proj1)
    summed2 = summed1 + proj1 * sig + emb[1]
    r2 = lax.rsqrt(mean_of(summed2 * summed2) + EPS)
    g2 = gpre[...]
    gsum = r2 * g2 - summed2 * (r2 * r2 * r2 * mean_of(g2 * summed2))
    emb[0] = gsum
    gproj = cot_ref[:, 0, :].astype(F32) + gsum * (sig * (1.0 + proj1 * (1.0 - sig)))
    g1 = back_through(gproj)
    summed1 = mixed[...]
    grad = emb[0] + r1 * g1 - summed1 * (r1 * r1 * r1 * mean_of(g1 * summed1))
    grad = pltpu.roll(grad, (1024 - shift) % 1024, 1)
    gb[x, yh] = grad.astype(BF16).reshape(2, 32, 1024)

    class Spread:
        def __init__(self, group):
            self.g, self.a, self.b = group, pl.ds(512 * group, 256), pl.ds(512 * group + 256, 256)
            self.y1 = (
                go.send(gb.at[x, yh, 0, :, self.b], grb.at[group, 0], yp),
                go.send(gb.at[x, yh, 1, :, self.b], grb.at[group, 1], ym),
            )
            own = gb.at[x, yh, :, :, self.a]
            self.x1 = (same(own, xp), same(own, xm))

        def second(self):
            for copy in self.y1:
                copy.wait_recv()
            self.y2 = (
                go.send(grb.at[self.g, 0], gb.at[x, at_y(-1) // 2, 0, :, self.b], yp),
                go.send(grb.at[self.g, 1], gb.at[x, at_y(1) // 2, 1, :, self.b], ym),
            )
            for copy in self.x1:
                copy.wait_recv()
            self.x2 = (
                same(gb.at[at_x(-1), yh, 0, :, self.a], xp),
                same(gb.at[at_x(1), yh, 1, :, self.a], xm),
            )

        def third(self):
            for copy in self.y2:
                copy.wait_recv()
            own = gb.at[x, :, :, :, self.b]
            self.bx1 = (same(own, xp), same(own, xm))
            for copy in self.x2:
                copy.wait_recv()
            self.ay1 = (
                go.send(gb.at[:, yh, 0, :, self.a], gra.at[self.g, 0], yp),
                go.send(gb.at[:, yh, 1, :, self.a], gra.at[self.g, 1], ym),
            )

        def fourth(self):
            for copy in self.bx1:
                copy.wait_recv()
            self.bx2 = (
                same(gb.at[at_x(-1), 0, :, :, self.b], xp),
                same(gb.at[at_x(1), 1, :, :, self.b], xm),
            )
            for copy in self.ay1:
                copy.wait_recv()
            self.ay2 = (
                go.send(gra.at[self.g, 0], gb.at[:, at_y(-1) // 2, 0, :, self.a], yp),
                go.send(gra.at[self.g, 1], gb.at[:, at_y(1) // 2, 1, :, self.a], ym),
            )

        def fifth(self):
            for copy in self.bx2 + self.ay2:
                copy.wait_recv()

    def weight_grad(j):
        block = gb[:, :, :, :, 256 * j:256 * j + 256].reshape(512, 256)
        wg[4 * j:4 * j + 4] = dot_tn(block, att[...]).astype(BF16).reshape(4, 2, 32, 512)

    def halves(group):
        weight_grad(2 * group)
        weight_grad(2 * group + 1)
        rows8 = pl.ds(8 * group, 8)
        return go.send(wg.at[rows8, 1 - c], wgr.at[rows8], mate)

    def own_chunk(rel):
        return wg[slot(rel), c].astype(F32) + wgr[slot(rel)].astype(F32)

    chains = ((8, 4), (7, 4), (-7, 4), (-6, 3))
    came = [None] * 4

    def chain_step(m):
        for n, (first, length) in enumerate(chains):
            if m >= length:
                continue
            sign = 1 if first > 0 else -1
            dist = first - 2 * sign * m
            value = own_chunk(dist)
            if m > 0:
                came[n].wait_recv()
                value = value + zrecv[n, m - 1].astype(F32)
            zsend[n, m] = value.astype(BF16)
            device = {2: zp2, 1: zp, -1: zm, -2: zm2}[max(-2, min(2, dist))]
            came[n] = go.send(zsend.at[n, m], zrecv.at[n, m], device)

    spread_far = Spread(1)
    spread_near = Spread(0)
    spread_far.second()
    spread_near.second()
    spread_far.third()
    spread_near.third()
    spread_far.fourth()
    spread_far.fifth()
    wg_far = halves(1)
    spread_near.fourth()
    wg_far.wait_recv()
    chain_step(0)
    spread_near.fifth()
    wg_near = halves(0)

    for j in range(2):
        total = None
        for zz in range(4):
            term = dot(
                gb[:, :, :, :, 256 * zz:256 * zz + 256].reshape(512, 256),
                proj[4 * zz:4 * zz + 4, :, :, 256 * j:256 * j + 256].reshape(256, 256),
            )
            total = term if total is None else total + term
        ga[:, 256 * j:256 * j + 256] = total.astype(BF16)

    for i in range(4):
        b_own[i] = dot_tn(q_ref[:, hs(i)], ga[:, hs(i)]).astype(BF16)
    back_copy = go.send(b_own, b_recv, mate)

    def backward(i):
        q0_, q1_ = q_ref[top, hs(i)], q_ref[bot, hs(i)]
        k0_, k1_ = k_ref[top, hs(i)], k_ref[bot, hs(i)]
        v0_, v1_ = v_ref[top, hs(i)], v_ref[bot, hs(i)]
        a0_, a1_ = ga[top, hs(i)], ga[bot, hs(i)]
        m00, m10, m11 = scores_of(ga, v_ref, i)
        e, b = s_in[i], b_in[i]
        gq_ref[top, hs(i)] = (scale * (dot(m00, k0_) + dot_nt(a0_, e))).astype(BF16)
        gq_ref[bot, hs(i)] = (
            scale * (dot(m10, k0_) + dot(m11, k1_) + dot_nt(a1_, e))
        ).astype(BF16)
        gk_ref[top, hs(i)] = (
            scale * (dot_tn(m00, q0_) + dot_tn(m10, q1_) + dot_nt(v0_, b))
        ).astype(BF16)
        gk_ref[bot, hs(i)] = (scale * (dot_tn(m11, q1_) + dot_nt(v1_, b))).astype(BF16)
        gv_ref[top, hs(i)] = (
            scale * (dot_tn(sc[i, 0], a0_) + dot_tn(sc[i, 1], a1_) + dot(k0_, b))
        ).astype(BF16)
        gv_ref[bot, hs(i)] = (scale * (dot_tn(sc[i, 2], a1_) + dot(k1_, b))).astype(BF16)

    chain_step(1)
    back_copy.wait_recv()
    bt_own[...] = (b_own[...].astype(F32) + b_recv[...].astype(F32)).astype(BF16)
    back_pair = go.send(bt_own, bt_recv, pair)
    wg_near.wait_recv()
    back_pair.wait_recv()
    b_in[...] = (
        (1.0 - cf) * b_recv[...].astype(F32) + (1.0 - ylf) * bt_recv[...].astype(F32)
    ).astype(BF16)
    backward(0)
    chain_step(2)
    backward(1)
    backward(2)
    chain_step(3)
    backward(3)
    total = own_chunk(0)
    for n, (first, length) in enumerate(chains):
        came[n].wait_recv()
        total = total + zrecv[n, length - 1].astype(F32)
    y_own[...] = total.astype(BF16)
    y_copy = go.send(y_own, y_recv, pair)
    y_copy.wait_recv()
    o_own[...] = y_own[...].astype(F32) + y_recv[...].astype(F32)
    o_copy = go.send(o_own, o_recv, mate)
    go_ref[pl.ds(pl.multiple_of(mine, 32), 32), :] = o_own[...]
    o_copy.wait_recv()
    go_ref[pl.ds(pl.multiple_of(32 - mine, 32), 32), :] = o_recv[...]
    go.drain()


def out_kernel(*refs):
    copies = [
        pltpu.make_async_copy(refs[n], refs[4 + n], refs[8].at[n]) for n in range(4)
    ]
    for copy in copies:
        copy.start()
    for copy in copies:
        copy.wait()


def write_out(*arrays):
    return pl.pallas_call(
        out_kernel,
        out_shape=tuple(jax.ShapeDtypeStruct(a.shape, a.dtype) for a in arrays),
        in_specs=[pl.BlockSpec(memory_space=pltpu.VMEM)] * 4,
        out_specs=(pl.BlockSpec(memory_space=pltpu.HBM),) * 4,
        scratch_shapes=[pltpu.SemaphoreType.DMA((4,))],
        compiler_params=pltpu.CompilerParams(vmem_limit_bytes=8 * 1024 * 1024),
        name="write_out",
    )(*arrays)


def on_device(queries, keys, values, out_proj, depth_proj, code_table, code_ids, depth_cotangent):
    scale = 2048.0 ** (-0.5)
    def vm(shape, kind=BF16):
        return pltpu.VMEM(shape, kind)

    state = vm((4, DH, DH))
    gq, gk, gv, gop = pl.pallas_call(
        functools.partial(kernel, scale),
        out_shape=(
            jax.ShapeDtypeStruct((512, 512), BF16),
            jax.ShapeDtypeStruct((512, 512), BF16),
            jax.ShapeDtypeStruct((512, 512), BF16),
            jax.ShapeDtypeStruct((64, 512), F32),
        ),
        in_specs=[pl.BlockSpec(memory_space=pltpu.HBM)] * 8,
        out_specs=(pl.BlockSpec(memory_space=pltpu.VMEM),) * 4,
        scratch_shapes=[
            vm((512, 512)), vm((512, 512)), vm((512, 512)), vm((64, 512)),
            vm((8, 1024)), vm((2, 8, 1024)), vm((2, 64), jnp.int32), vm((64, 2, 1024)),
            pltpu.SemaphoreType.DMA((8,)),
            vm((16, 3, 16, 128)), vm((16, 2, 32, 512)), vm((3, 4, 2, 2, 64, 1024)),
            state, state, state, state, state,
            state, state, state, state, state,
            vm((4, 3, 256, 256)), vm((512, 512), F32), vm((512, 512)),
            vm((4, 2, 2, 32, 1024)),
            vm((2, 2, 32, 256)), vm((2, 2, 32, 256)),
            vm((2, 2, 2, 32, 256)), vm((2, 2, 2, 32, 256)),
            vm((2, 2, 32, 256)), vm((2, 2, 32, 256)), vm((2, 2, 32, 256)),
            vm((2, 2, 4, 32, 256)), vm((2, 2, 4, 32, 256)),
            vm((2, 4, 2, 32, 256)), vm((2, 2, 32, 256)), vm((2, 2, 2, 32, 256)),
            vm((64, 1024), F32), vm((2, 64, 1024), F32), vm((64, 1024), F32),
            vm((4, 2, 2, 32, 1024)), vm((2, 2, 4, 32, 256)), vm((2, 2, 32, 256)),
            vm((512, 512)), vm((16, 2, 32, 512)), vm((16, 32, 512)),
            vm((4, 4, 32, 512)), vm((4, 4, 32, 512)),
            vm((32, 512)), vm((32, 512)), vm((32, 512), F32), vm((32, 512), F32),
            pltpu.SemaphoreType.DMA((N_COPIES,)),
            pltpu.SemaphoreType.DMA((N_COPIES,)),
        ],
        compiler_params=pltpu.CompilerParams(
            collective_id=0, has_side_effects=True, vmem_limit_bytes=34 * 1024 * 1024
        ),
        name="fused_step",
    )(
        *(
            pltpu.with_memory_space_constraint(array, pltpu.HBM)
            for array in (
                queries[0], keys[0], values[0], out_proj.T, depth_proj.T, code_table,
                code_ids[0].T, depth_cotangent[0],
            )
        )
    )
    gq, gk, gv, gop = write_out(gq, gk, gv, gop)
    return gq[None], gk[None], gv[None], gop.T


def solution(mesh):
    in_specs = (
        P("dp", "seq", "head"),
        P("dp", "seq", "head"),
        P("dp", "seq", "head"),
        P("head", "dp"),
        P(None, ("head", "dp")),
        P(None, ("head", "dp"), None),
        P("dp", ("seq", "head"), None),
        P("dp", ("seq", "head"), None, None),
    )
    out_specs = (
        P("dp", "seq", "head"),
        P("dp", "seq", "head"),
        P("dp", "seq", "head"),
        P("head", "dp"),
    )
    return jax.shard_map(
        on_device, mesh=mesh, in_specs=in_specs, out_specs=out_specs, check_vma=False
    )
```

```python
import functools

import jax
import jax.numpy as jnp
from jax import lax
from jax.experimental import pallas as pl
from jax.experimental.pallas import tpu as pltpu
from jax.sharding import PartitionSpec as P

DH = 128
F32 = jnp.float32
BF16 = jnp.bfloat16
EPS = 1e-05
HALF = 256
N_COPIES = 256


def dot(a, b):
    return lax.dot_general(a, b, (((1,), (0,)), ((), ())), preferred_element_type=F32)


def dot_nt(a, b):
    return lax.dot_general(a, b, (((1,), (1,)), ((), ())), preferred_element_type=F32)


def dot_tn(a, b):
    return lax.dot_general(a, b, (((0,), (0,)), ((), ())), preferred_element_type=F32)


class Copies:
    def __init__(self, send_sems, recv_sems):
        self.send_sems, self.recv_sems, self.all = send_sems, recv_sems, []

    def send(self, src, dst, device):
        index = len(self.all)
        copy = pltpu.make_async_remote_copy(
            src_ref=src,
            dst_ref=dst,
            send_sem=self.send_sems.at[index],
            recv_sem=self.recv_sems.at[index],
            device_id=device,
            device_id_type=pl.DeviceIdType.MESH,
        )
        copy.start()
        self.all.append(copy)
        return copy

    def drain(self):
        for copy in self.all:
            copy.wait_send()


def kernel(
    scale,
    q_in, k_in, v_in, op_in, dp_in, tab_in, ids_in, cot_in,
    gq_ref, gk_ref, gv_ref, go_ref,
    q_ref, k_ref, v_ref, op_ref, dp_ref, tab_ref, ids_ref, cot_ref, load_sems,
    wz, proj, wts,
    s_own, s_recv, t_own, t_recv, s_in,
    b_own, b_recv, bt_own, bt_recv, b_in,
    sc, acc, att,
    mix, ra1, rb1, ra2, rb2, ray, rar, raf, rbr, rbf, yb, sb1, sb2,
    mixed, emb, gpre,
    gb, gra, grb,
    ga, wg, wgr, zsend, zrecv, y_own, y_recv,
    send_sems, recv_sems,
):
    seq, head, z = lax.axis_index("seq"), lax.axis_index("head"), lax.axis_index("dp")
    x, yh, yl, c = head // 2, head % 2, seq // 2, seq % 2
    y = 2 * yh + yl
    nz = 16

    def at_x(step):
        return (x + step + 4) % 4

    def at_y(step):
        return (y + step + 4) % 4

    def at_z(step):
        return (z + step + nz) % nz

    def dev(x_=None, y_=None, z_=None, c_=None):
        x_ = x if x_ is None else x_
        y_ = y if y_ is None else y_
        z_ = z if z_ is None else z_
        c_ = c if c_ is None else c_
        return {"seq": 2 * (y_ % 2) + c_, "head": 2 * x_ + y_ // 2, "dp": z_}

    xp, xm = dev(x_=at_x(1)), dev(x_=at_x(-1))
    yp, ym = dev(y_=at_y(1)), dev(y_=at_y(-1))
    zp, zm = dev(z_=at_z(1)), dev(z_=at_z(-1))
    zp2, zm2 = dev(z_=at_z(2)), dev(z_=at_z(-2))
    mate = dev(c_=1 - c)
    pair = dev(y_=2 * yh + 1 - yl)
    cross = dev(y_=2 * yh + 1 - yl, c_=1 - c)
    cf, ylf = c.astype(F32), yl.astype(F32)
    go = Copies(send_sems, recv_sems)

    barrier = pltpu.get_barrier_semaphore()
    for other in (xp, xm, yp, ym, zp, zm, zp2, zm2, mate, cross):
        pl.semaphore_signal(barrier, inc=1, device_id=other, device_id_type=pl.DeviceIdType.MESH)

    def hs(i):
        return slice(i * DH, (i + 1) * DH)

    loads = [
        pltpu.make_async_copy(src, dst, load_sems.at[n])
        for n, (src, dst) in enumerate((
            (dp_in, dp_ref), (tab_in, tab_ref), (k_in, k_ref), (v_in, v_ref),
            (q_in, q_ref), (op_in, op_ref), (ids_in, ids_ref), (cot_in, cot_ref),
        ))
    ]
    for load in loads:
        load.start()
    quarter = 2 * c + yl
    loads[0].wait()
    loads[1].wait()
    mine = c * 32
    qown = pl.ds(pl.multiple_of(quarter * 256, 256), 256)
    for a in range(3):
        rows8 = (dp_ref[:, qown] if a == 0 else tab_ref[a - 1, :, qown]).astype(F32)
        wz[3, a] = jnp.concatenate([rows8[:, :128], rows8[:, 128:]], axis=0).astype(BF16)
    loads[2].wait()
    loads[3].wait()
    for i in range(4):
        s_own[i] = dot_tn(k_ref[:, hs(i)], v_ref[:, hs(i)]).astype(BF16)
    for load in loads[4:]:
        load.wait()
    pl.semaphore_wait(barrier, 10)

    state_copy = go.send(s_own, s_recv, mate)
    own_p = op_ref.at[pl.ds(pl.multiple_of(mine, 32), 32), :]

    w_came, p_came, to_mate = {}, {}, {}

    def slot(rel):
        return (rel + 3) % nz

    def send_wz(rel, hop, device):
        w_came[rel - hop] = go.send(wz.at[slot(rel)], wz.at[slot(rel - hop)], device)

    def send_p(rel, hop, device):
        src = own_p if rel == 0 else proj.at[slot(rel), c]
        p_came[rel - hop] = go.send(src, proj.at[slot(rel - hop), c], device)

    def p_mate(rel):
        window = proj.at[slot(rel), c]
        to_mate[rel] = go.send(window, window, mate)

    around = ((1, zp), (-1, zm), (2, zp2), (-2, zm2))
    for hop, device in around:
        send_wz(0, hop, device)
    for hop, device in around:
        send_p(0, hop, device)
    proj[3] = op_ref[...].reshape(2, 32, 512)

    def relay_w(j):
        for sign, device in ((-1, zp2), (1, zm2)):
            for rel in (sign * (2 * j - 1), sign * 2 * j):
                w_came[rel].wait_recv()
                if rel != 6:
                    send_wz(rel, -2 * sign, device)

    def relay_p(j):
        for sign, device in ((-1, zp2), (1, zm2)):
            for rel in (sign * (2 * j - 1), sign * 2 * j):
                p_came[rel].wait_recv()
                if rel != 6:
                    send_p(rel, -2 * sign, device)
        for sign in (-1, 1):
            for rel in (sign * (2 * j - 1), sign * 2 * j):
                p_mate(rel)

    rows = lax.broadcasted_iota(jnp.int32, (HALF, HALF), 0)
    cols = lax.broadcasted_iota(jnp.int32, (HALF, HALF), 1)
    low = rows >= cols
    top, bot = slice(0, HALF), slice(HALF, 2 * HALF)

    def scores_of(a_ref, b_ref, i):
        a0, a1 = a_ref[top, hs(i)], a_ref[bot, hs(i)]
        b0, b1 = b_ref[top, hs(i)], b_ref[bot, hs(i)]
        m00 = jnp.where(low, dot_nt(a0, b0), 0.0).astype(BF16)
        m10 = dot_nt(a1, b0).astype(BF16)
        m11 = jnp.where(low, dot_nt(a1, b1), 0.0).astype(BF16)
        return m00, m10, m11

    def forward(i):
        m00, m10, m11 = scores_of(q_ref, k_ref, i)
        sc[i, 0], sc[i, 1], sc[i, 2] = m00, m10, m11
        v0, v1 = v_ref[top, hs(i)], v_ref[bot, hs(i)]
        acc[top, hs(i)] = dot(m00, v0)
        acc[bot, hs(i)] = dot(m10, v0) + dot(m11, v1)

    def pass_state():
        state_copy.wait_recv()
        t_own[...] = (s_own[...].astype(F32) + s_recv[...].astype(F32)).astype(BF16)
        return go.send(t_own, t_recv, pair)

    def finish_attended():
        pair_copy.wait_recv()
        s_in[...] = (cf * s_recv[...].astype(F32) + ylf * t_recv[...].astype(F32)).astype(BF16)
        for i in range(4):
            att[:, hs(i)] = (
                scale * (acc[:, hs(i)] + dot(q_ref[:, hs(i)], s_in[i]))
            ).astype(BF16)

    q0 = pl.multiple_of(quarter * 256, 256)
    ccols = pl.ds(pl.multiple_of(c * 512, 512), 512)

    def qcols(y_):
        return pl.ds(pl.multiple_of((2 * c + y_ % 2) * 256, 256), 256)

    def same(win, device):
        return go.send(win, win, device)

    w_mate = []

    class Plane:
        def __init__(self, group):
            self.g = group
            for a in range(3):
                block = wz[group * 8:group * 8 + 8, a].astype(F32)
                piece = jnp.concatenate(
                    [block[:, :8].reshape(64, 128), block[:, 8:].reshape(64, 128)], axis=1
                )
                wts[a, x, yh, group, :, pl.ds(q0, 256)] = piece.astype(BF16)
            self.wait_for = (
                same(self.ax(x, 0, 32), xp), same(self.ax(x, 0, 32), xm),
                same(self.by(y, 32, 32), yp), same(self.by(y, 32, 32), ym),
            )

        def ax(self, xx, r0, n):
            return wts.at[:, xx, yh, self.g, pl.ds(r0, n), qcols(y)]

        def by(self, yy, r0, n):
            return wts.at[:, x, yy // 2, self.g, pl.ds(r0, n), qcols(yy)]

        def ay(self, yy, r0, n):
            return wts.at[:, :, yy // 2, self.g, pl.ds(r0, n), qcols(yy)]

        def bx(self, xx, r0, n):
            return wts.at[:, xx, :, self.g, pl.ds(r0, n), ccols]

        def arrived(self):
            for copy in self.wait_for:
                copy.wait_recv()

        def second(self):
            self.arrived()
            self.wait_for = (
                same(self.ax(at_x(-1), 0, 16), xp), same(self.ax(at_x(1), 16, 16), xm),
                same(self.by(at_y(-1), 32, 16), yp), same(self.by(at_y(1), 48, 16), ym),
            )

        def third(self):
            self.arrived()
            self.wait_for = (
                same(self.ay(y, 0, 32), yp), same(self.ay(y, 0, 32), ym),
                same(self.bx(x, 32, 32), xp), same(self.bx(x, 32, 32), xm),
            )
            w_mate.append(same(self.ay(y, 0, 32), mate))
            w_mate.append(same(self.bx(x, 32, 32), mate))

        def fourth(self):
            self.arrived()
            self.wait_for = (
                same(self.ay(at_y(-1), 0, 16), yp), same(self.ay(at_y(1), 16, 16), ym),
                same(self.bx(at_x(-1), 32, 16), xp), same(self.bx(at_x(1), 48, 16), xm),
            )
            for step in (-1, 1):
                w_mate.append(same(self.ay(at_y(step), 0, 32), mate))
                w_mate.append(same(self.bx(at_x(step), 32, 32), mate))

        def fifth(self):
            self.arrived()
            w_mate.append(same(self.ay(at_y(2), 0, 32), mate))
            w_mate.append(same(self.bx(at_x(2), 32, 32), mate))

    class Reduce:
        def __init__(self, group):
            self.g, self.a0, self.b0 = group, 512 * group, 512 * group + 256
            self.block(2 * group + 1)
            b = pl.ds(self.b0, 256)
            self.y1 = (
                go.send(mix.at[:, 1 - yh, 0, :, b], rbr.at[group, 0], yp),
                go.send(mix.at[:, 1 - yh, 1, :, b], rbr.at[group, 1], ym),
            )
            self.block(2 * group)
            a = pl.ds(self.a0, 256)
            self.x1 = (
                go.send(mix.at[at_x(2), 0, :, :, a], ra1.at[group], xp),
                go.send(mix.at[at_x(2), 1, :, :, a], rb1.at[group], xm),
            )

        def block(self, j):
            part = dot_nt(att[...], proj[4 * j:4 * j + 4].reshape(256, 512))
            mix[:, :, :, :, 256 * j:256 * j + 256] = part.astype(BF16).reshape(4, 2, 2, 32, 256)

        def second(self):
            g, al = self.g, slice(self.a0, self.a0 + 256)
            for copy in self.y1:
                copy.wait_recv()
            self.y2 = (
                go.send(rbr.at[g, 0], rbf.at[g, 0], yp), go.send(rbr.at[g, 1], rbf.at[g, 1], ym)
            )
            for copy in self.x1:
                copy.wait_recv()
            mix[at_x(1), 0, :, :, al] = (
                mix[at_x(1), 0, :, :, al].astype(F32) + ra1[g].astype(F32)
            ).astype(BF16)
            mix[at_x(-1), 1, :, :, al] = (
                mix[at_x(-1), 1, :, :, al].astype(F32) + rb1[g].astype(F32)
            ).astype(BF16)
            a = pl.ds(self.a0, 256)
            self.x2 = (
                go.send(mix.at[at_x(1), :, :, :, a], ra2.at[g], xp),
                go.send(mix.at[at_x(-1), :, :, :, a], rb2.at[g], xm),
            )

        def third(self):
            g, al, be = self.g, slice(self.a0, self.a0 + 256), slice(self.b0, self.b0 + 256)
            for copy in self.y2:
                copy.wait_recv()
            for hf in range(2):
                yb[g, :, hf] = (
                    mix[:, yh, hf, :, be].astype(F32) + rbf[g, hf].astype(F32)
                ).astype(BF16)
            self.bx1 = (
                go.send(yb.at[g, at_x(2), 0], sb1.at[g, 0], xp),
                go.send(yb.at[g, at_x(2), 1], sb1.at[g, 1], xm),
            )
            for copy in self.x2:
                copy.wait_recv()
            ray[g] = (
                mix[x, 1 - yh, :, :, al].astype(F32)
                + ra2[g, 1 - yh].astype(F32)
                + rb2[g, 1 - yh].astype(F32)
            ).astype(BF16)
            self.ay1 = (
                go.send(ray.at[g, 0], rar.at[g, 0], yp), go.send(ray.at[g, 1], rar.at[g, 1], ym)
            )
            mixed[:, al] = (
                mix[x, yh, :, :, al].astype(F32)
                + ra2[g, yh].astype(F32)
                + rb2[g, yh].astype(F32)
            ).reshape(64, 256)

        def fourth(self):
            g = self.g
            for copy in self.bx1:
                copy.wait_recv()
            for step, hf in ((1, 0), (-1, 1)):
                yb[g, at_x(step), hf] = (
                    yb[g, at_x(step), hf].astype(F32) + sb1[g, hf].astype(F32)
                ).astype(BF16)
            self.bx2 = (
                go.send(yb.at[g, at_x(1)], sb2.at[g, 0], xp),
                go.send(yb.at[g, at_x(-1)], sb2.at[g, 1], xm),
            )
            for copy in self.ay1:
                copy.wait_recv()
            self.ay2 = (
                go.send(rar.at[g, 0], raf.at[g, 0], yp), go.send(rar.at[g, 1], raf.at[g, 1], ym)
            )

        def fifth(self):
            g, al, be = self.g, slice(self.a0, self.a0 + 256), slice(self.b0, self.b0 + 256)
            for copy in self.ay2 + self.bx2:
                copy.wait_recv()
            mixed[:, al] = mixed[:, al] + raf[g].astype(F32).reshape(64, 256)
            mixed[:, be] = (
                yb[g, x].astype(F32) + sb2[g, 0].astype(F32) + sb2[g, 1].astype(F32)
            ).reshape(64, 256)

    forward(0)
    pair_copy = pass_state()
    forward(1)
    relay_w(1)
    relay_p(1)
    forward(2)
    forward(3)
    relay_w(2)
    near = Plane(0)
    relay_p(2)
    finish_attended()
    relay_w(3)
    near.second()
    for rel in (-1, -2, 1, 2, -3, 3, 4):
        to_mate[rel].wait_recv()
    mnear = Reduce(0)
    relay_p(3)
    near.third()
    mnear.second()
    for rel in (-7, -8, 7):
        w_came[rel].wait_recv()
    far = Plane(1)
    for rel in (-7, -8, 7):
        p_came[rel].wait_recv()
        p_mate(rel)
    near.fourth()
    for rel in (-4, -5, -6, 5, 6, -7, -8, 7):
        to_mate[rel].wait_recv()
    mfar = Reduce(1)
    mnear.third()
    far.second()
    mfar.second()
    far.third()
    mnear.fourth()
    near.fifth()
    mfar.third()
    mnear.fifth()
    mfar.fourth()
    far.fourth()
    mfar.fifth()
    far.fifth()
    for copy in w_mate:
        copy.wait_recv()

    def weight(a, xx):
        return wts[a, xx].reshape(256, 1024)

    turn = (z * 8 + 128 - 24) % 128
    place = lax.broadcasted_iota(jnp.int32, (256, 64), 0)
    vocab = place - place % 128 + (place % 128 + turn) % 128
    for level in range(2):
        ids = ids_ref[level:level + 1, :]
        total = None
        for xx in range(4):
            onehot = jnp.where(ids - 256 * xx == vocab, 1.0, 0.0).astype(BF16)
            term = dot_tn(onehot, weight(1 + level, xx))
            total = term if total is None else total + term
        emb[level] = total

    def turned(value, by):
        return jnp.concatenate(
            [pltpu.roll(value[:, 128 * j:128 * j + 128], by, 1) for j in range(8)], axis=1
        )

    def back_through(g):
        g = turned(g, (128 - turn) % 128).astype(BF16)
        total = None
        for xx in range(4):
            term = dot(g[:, 256 * xx:256 * xx + 256], weight(0, xx))
            total = term if total is None else total + term
        return total

    gpre[...] = back_through(cot_ref[:, 1, :].astype(F32))

    def mean_of(value):
        return jnp.mean(value, axis=-1, keepdims=True)

    shift = (z * 64 + 1024 - 192) % 1024
    summed1 = pltpu.roll(mixed[...], shift, 1) + emb[0]
    r1 = lax.rsqrt(mean_of(summed1 * summed1) + EPS)
    normed1 = (summed1 * r1).astype(BF16)
    mixed[...] = summed1
    proj1 = turned(
        jnp.concatenate([dot_nt(normed1, weight(0, xx)) for xx in range(4)], axis=1), turn
    )
    sig = jax.nn.sigmoid(proj1)
    summed2 = summed1 + proj1 * sig + emb[1]
    r2 = lax.rsqrt(mean_of(summed2 * summed2) + EPS)
    g2 = gpre[...]
    gsum = r2 * g2 - summed2 * (r2 * r2 * r2 * mean_of(g2 * summed2))
    emb[0] = gsum
    gproj = cot_ref[:, 0, :].astype(F32) + gsum * (sig * (1.0 + proj1 * (1.0 - sig)))
    g1 = back_through(gproj)
    summed1 = mixed[...]
    grad = emb[0] + r1 * g1 - summed1 * (r1 * r1 * r1 * mean_of(g1 * summed1))
    grad = pltpu.roll(grad, (1024 - shift) % 1024, 1)
    gb[x, yh] = grad.astype(BF16).reshape(2, 32, 1024)

    class Spread:
        def __init__(self, group):
            self.g, self.a, self.b = group, pl.ds(512 * group, 256), pl.ds(512 * group + 256, 256)
            self.y1 = (
                go.send(gb.at[x, yh, 0, :, self.b], grb.at[group, 0], yp),
                go.send(gb.at[x, yh, 1, :, self.b], grb.at[group, 1], ym),
            )
            own = gb.at[x, yh, :, :, self.a]
            self.x1 = (same(own, xp), same(own, xm))

        def second(self):
            for copy in self.y1:
                copy.wait_recv()
            self.y2 = (
                go.send(grb.at[self.g, 0], gb.at[x, at_y(-1) // 2, 0, :, self.b], yp),
                go.send(grb.at[self.g, 1], gb.at[x, at_y(1) // 2, 1, :, self.b], ym),
            )
            for copy in self.x1:
                copy.wait_recv()
            self.x2 = (
                same(gb.at[at_x(-1), yh, 0, :, self.a], xp),
                same(gb.at[at_x(1), yh, 1, :, self.a], xm),
            )

        def third(self):
            for copy in self.y2:
                copy.wait_recv()
            own = gb.at[x, :, :, :, self.b]
            self.bx1 = (same(own, xp), same(own, xm))
            for copy in self.x2:
                copy.wait_recv()
            self.ay1 = (
                go.send(gb.at[:, yh, 0, :, self.a], gra.at[self.g, 0], yp),
                go.send(gb.at[:, yh, 1, :, self.a], gra.at[self.g, 1], ym),
            )

        def fourth(self):
            for copy in self.bx1:
                copy.wait_recv()
            self.bx2 = (
                same(gb.at[at_x(-1), 0, :, :, self.b], xp),
                same(gb.at[at_x(1), 1, :, :, self.b], xm),
            )
            for copy in self.ay1:
                copy.wait_recv()
            self.ay2 = (
                go.send(gra.at[self.g, 0], gb.at[:, at_y(-1) // 2, 0, :, self.a], yp),
                go.send(gra.at[self.g, 1], gb.at[:, at_y(1) // 2, 1, :, self.a], ym),
            )

        def fifth(self):
            for copy in self.bx2 + self.ay2:
                copy.wait_recv()

    def weight_grad(j):
        block = gb[:, :, :, :, 256 * j:256 * j + 256].reshape(512, 256)
        wg[4 * j:4 * j + 4] = dot_tn(block, att[...]).astype(BF16).reshape(4, 2, 32, 512)

    def halves(group):
        weight_grad(2 * group)
        weight_grad(2 * group + 1)
        rows8 = pl.ds(8 * group, 8)
        return go.send(wg.at[rows8, 1 - c], wgr.at[rows8], mate)

    def own_chunk(rel):
        return wg[slot(rel), c].astype(F32) + wgr[slot(rel)].astype(F32)

    chains = ((8, 4), (7, 4), (-7, 4), (-6, 3))
    came = [None] * 4

    def chain_step(m):
        for n, (first, length) in enumerate(chains):
            if m >= length:
                continue
            sign = 1 if first > 0 else -1
            dist = first - 2 * sign * m
            value = own_chunk(dist)
            if m > 0:
                came[n].wait_recv()
                value = value + zrecv[n, m - 1].astype(F32)
            zsend[n, m] = value.astype(BF16)
            device = {2: zp2, 1: zp, -1: zm, -2: zm2}[max(-2, min(2, dist))]
            came[n] = go.send(zsend.at[n, m], zrecv.at[n, m], device)

    spread_far = Spread(1)
    spread_far.second()
    spread_near = Spread(0)
    spread_far.third()
    spread_near.second()
    spread_far.fourth()
    spread_near.third()
    spread_far.fifth()
    wg_far = halves(1)
    spread_near.fourth()
    wg_far.wait_recv()
    chain_step(0)
    spread_near.fifth()
    chain_step(1)
    wg_near = halves(0)

    for j in range(2):
        total = None
        for zz in range(4):
            term = dot(
                gb[:, :, :, :, 256 * zz:256 * zz + 256].reshape(512, 256),
                proj[4 * zz:4 * zz + 4, :, :, 256 * j:256 * j + 256].reshape(256, 256),
            )
            total = term if total is None else total + term
        ga[:, 256 * j:256 * j + 256] = total.astype(BF16)

    for i in range(4):
        b_own[i] = dot_tn(q_ref[:, hs(i)], ga[:, hs(i)]).astype(BF16)
    back_copy = go.send(b_own, b_recv, mate)

    def backward(i):
        q0_, q1_ = q_ref[top, hs(i)], q_ref[bot, hs(i)]
        k0_, k1_ = k_ref[top, hs(i)], k_ref[bot, hs(i)]
        v0_, v1_ = v_ref[top, hs(i)], v_ref[bot, hs(i)]
        a0_, a1_ = ga[top, hs(i)], ga[bot, hs(i)]
        m00, m10, m11 = scores_of(ga, v_ref, i)
        e, b = s_in[i], b_in[i]
        gq_ref[top, hs(i)] = (scale * (dot(m00, k0_) + dot_nt(a0_, e))).astype(BF16)
        gq_ref[bot, hs(i)] = (
            scale * (dot(m10, k0_) + dot(m11, k1_) + dot_nt(a1_, e))
        ).astype(BF16)
        gk_ref[top, hs(i)] = (
            scale * (dot_tn(m00, q0_) + dot_tn(m10, q1_) + dot_nt(v0_, b))
        ).astype(BF16)
        gk_ref[bot, hs(i)] = (scale * (dot_tn(m11, q1_) + dot_nt(v1_, b))).astype(BF16)
        gv_ref[top, hs(i)] = (
            scale * (dot_tn(sc[i, 0], a0_) + dot_tn(sc[i, 1], a1_) + dot(k0_, b))
        ).astype(BF16)
        gv_ref[bot, hs(i)] = (scale * (dot_tn(sc[i, 2], a1_) + dot(k1_, b))).astype(BF16)

    back_copy.wait_recv()
    bt_own[...] = (b_own[...].astype(F32) + b_recv[...].astype(F32)).astype(BF16)
    back_pair = go.send(bt_own, bt_recv, pair)
    wg_near.wait_recv()
    chain_step(2)
    back_pair.wait_recv()
    b_in[...] = (
        (1.0 - cf) * b_recv[...].astype(F32) + (1.0 - ylf) * bt_recv[...].astype(F32)
    ).astype(BF16)
    backward(0)
    backward(1)
    backward(2)
    chain_step(3)
    backward(3)
    total = own_chunk(0)
    for n, (first, length) in enumerate(chains):
        came[n].wait_recv()
        total = total + zrecv[n, length - 1].astype(F32)
    y_own[...] = total.astype(BF16)
    last = [go.send(y_own, y_recv.at[n], device) for n, device in enumerate((pair, mate, cross))]
    for copy in last:
        copy.wait_recv()
    go_ref[pl.ds(pl.multiple_of(mine, 32), 32), :] = (
        y_own[...].astype(F32) + y_recv[0].astype(F32)
    )
    go_ref[pl.ds(pl.multiple_of(32 - mine, 32), 32), :] = (
        y_recv[1].astype(F32) + y_recv[2].astype(F32)
    )
    go.drain()


def out_kernel(*refs):
    copies = [
        pltpu.make_async_copy(refs[n], refs[4 + n], refs[8].at[n]) for n in range(4)
    ]
    for copy in copies:
        copy.start()
    for copy in copies:
        copy.wait()


def write_out(*arrays):
    return pl.pallas_call(
        out_kernel,
        out_shape=tuple(jax.ShapeDtypeStruct(a.shape, a.dtype) for a in arrays),
        in_specs=[pl.BlockSpec(memory_space=pltpu.VMEM)] * 4,
        out_specs=(pl.BlockSpec(memory_space=pltpu.HBM),) * 4,
        scratch_shapes=[pltpu.SemaphoreType.DMA((4,))],
        compiler_params=pltpu.CompilerParams(vmem_limit_bytes=8 * 1024 * 1024),
        name="write_out",
    )(*arrays)


def on_device(queries, keys, values, out_proj, depth_proj, code_table, code_ids, depth_cotangent):
    scale = 2048.0 ** (-0.5)
    def vm(shape, kind=BF16):
        return pltpu.VMEM(shape, kind)

    state = vm((4, DH, DH))
    gq, gk, gv, gop = pl.pallas_call(
        functools.partial(kernel, scale),
        out_shape=(
            jax.ShapeDtypeStruct((512, 512), BF16),
            jax.ShapeDtypeStruct((512, 512), BF16),
            jax.ShapeDtypeStruct((512, 512), BF16),
            jax.ShapeDtypeStruct((64, 512), F32),
        ),
        in_specs=[pl.BlockSpec(memory_space=pltpu.HBM)] * 8,
        out_specs=(pl.BlockSpec(memory_space=pltpu.VMEM),) * 4,
        scratch_shapes=[
            vm((512, 512)), vm((512, 512)), vm((512, 512)), vm((64, 512)),
            vm((8, 1024)), vm((2, 8, 1024)), vm((2, 64), jnp.int32), vm((64, 2, 1024)),
            pltpu.SemaphoreType.DMA((8,)),
            vm((16, 3, 16, 128)), vm((16, 2, 32, 512)), vm((3, 4, 2, 2, 64, 1024)),
            state, state, state, state, state,
            state, state, state, state, state,
            vm((4, 3, 256, 256)), vm((512, 512), F32), vm((512, 512)),
            vm((4, 2, 2, 32, 1024)),
            vm((2, 2, 32, 256)), vm((2, 2, 32, 256)),
            vm((2, 2, 2, 32, 256)), vm((2, 2, 2, 32, 256)),
            vm((2, 2, 32, 256)), vm((2, 2, 32, 256)), vm((2, 2, 32, 256)),
            vm((2, 2, 4, 32, 256)), vm((2, 2, 4, 32, 256)),
            vm((2, 4, 2, 32, 256)), vm((2, 2, 32, 256)), vm((2, 2, 2, 32, 256)),
            vm((64, 1024), F32), vm((2, 64, 1024), F32), vm((64, 1024), F32),
            vm((4, 2, 2, 32, 1024)), vm((2, 2, 4, 32, 256)), vm((2, 2, 32, 256)),
            vm((512, 512)), vm((16, 2, 32, 512)), vm((16, 32, 512)),
            vm((4, 4, 32, 512)), vm((4, 4, 32, 512)),
            vm((32, 512)), vm((3, 32, 512)),
            pltpu.SemaphoreType.DMA((N_COPIES,)),
            pltpu.SemaphoreType.DMA((N_COPIES,)),
        ],
        compiler_params=pltpu.CompilerParams(
            collective_id=0, has_side_effects=True, vmem_limit_bytes=34 * 1024 * 1024
        ),
        name="fused_step",
    )(
        *(
            pltpu.with_memory_space_constraint(array, pltpu.HBM)
            for array in (
                queries[0], keys[0], values[0], out_proj.T, depth_proj.T, code_table,
                code_ids[0].T, depth_cotangent[0],
            )
        )
    )
    gq, gk, gv, gop = write_out(gq, gk, gv, gop)
    return gq[None], gk[None], gv[None], gop.T


def solution(mesh):
    in_specs = (
        P("dp", "seq", "head"),
        P("dp", "seq", "head"),
        P("dp", "seq", "head"),
        P("head", "dp"),
        P(None, ("head", "dp")),
        P(None, ("head", "dp"), None),
        P("dp", ("seq", "head"), None),
        P("dp", ("seq", "head"), None, None),
    )
    out_specs = (
        P("dp", "seq", "head"),
        P("dp", "seq", "head"),
        P("dp", "seq", "head"),
        P("head", "dp"),
    )
    return jax.shard_map(
        on_device, mesh=mesh, in_specs=in_specs, out_specs=out_specs, check_vma=False
    )
```

```python
import functools

import jax
import jax.numpy as jnp
from jax import lax
from jax.experimental import pallas as pl
from jax.experimental.pallas import tpu as pltpu
from jax.sharding import PartitionSpec as P

DH = 128
F32 = jnp.float32
BF16 = jnp.bfloat16
EPS = 1e-05
HALF = 256
N_COPIES = 256


def dot(a, b):
    return lax.dot_general(a, b, (((1,), (0,)), ((), ())), preferred_element_type=F32)


def dot_nt(a, b):
    return lax.dot_general(a, b, (((1,), (1,)), ((), ())), preferred_element_type=F32)


def dot_tn(a, b):
    return lax.dot_general(a, b, (((0,), (0,)), ((), ())), preferred_element_type=F32)


class Copies:
    def __init__(self, send_sems, recv_sems):
        self.send_sems, self.recv_sems, self.all = send_sems, recv_sems, []

    def send(self, src, dst, device):
        index = len(self.all)
        copy = pltpu.make_async_remote_copy(
            src_ref=src,
            dst_ref=dst,
            send_sem=self.send_sems.at[index],
            recv_sem=self.recv_sems.at[index],
            device_id=device,
            device_id_type=pl.DeviceIdType.MESH,
        )
        copy.start()
        self.all.append(copy)
        return copy

    def drain(self):
        for copy in self.all:
            copy.wait_send()


def kernel(
    scale,
    q_in, k_in, v_in, op_in, dp_in, tab_in, ids_in, cot_in,
    gq_ref, gk_ref, gv_ref, go_ref,
    q_ref, k_ref, v_ref, op_ref, dp_ref, tab_ref, ids_ref, cot_ref, load_sems,
    wz, proj, wts,
    s_own, s_recv, t_own, t_recv, s_in,
    b_own, b_recv, bt_own, bt_recv, b_in,
    sc, acc, att,
    mix, ra1, rb1, ra2, rb2, ray, rar, raf, rbr, rbf, yb, sb1, sb2,
    mixed, emb, gpre,
    gb, gra, grb,
    ga, wg, wgr, zsend, zrecv, y_own, y_recv,
    send_sems, recv_sems,
):
    seq, head, z = lax.axis_index("seq"), lax.axis_index("head"), lax.axis_index("dp")
    x, yh, yl, c = head // 2, head % 2, seq // 2, seq % 2
    y = 2 * yh + yl
    nz = 16

    def at_x(step):
        return (x + step + 4) % 4

    def at_y(step):
        return (y + step + 4) % 4

    def at_z(step):
        return (z + step + nz) % nz

    def dev(x_=None, y_=None, z_=None, c_=None):
        x_ = x if x_ is None else x_
        y_ = y if y_ is None else y_
        z_ = z if z_ is None else z_
        c_ = c if c_ is None else c_
        return {"seq": 2 * (y_ % 2) + c_, "head": 2 * x_ + y_ // 2, "dp": z_}

    xp, xm = dev(x_=at_x(1)), dev(x_=at_x(-1))
    yp, ym = dev(y_=at_y(1)), dev(y_=at_y(-1))
    zp, zm = dev(z_=at_z(1)), dev(z_=at_z(-1))
    zp2, zm2 = dev(z_=at_z(2)), dev(z_=at_z(-2))
    mate = dev(c_=1 - c)
    pair = dev(y_=2 * yh + 1 - yl)
    cross = dev(y_=2 * yh + 1 - yl, c_=1 - c)
    cf, ylf = c.astype(F32), yl.astype(F32)
    go = Copies(send_sems, recv_sems)

    barrier = pltpu.get_barrier_semaphore()
    for other in (xp, xm, yp, ym, zp, zm, zp2, zm2, mate, cross):
        pl.semaphore_signal(barrier, inc=1, device_id=other, device_id_type=pl.DeviceIdType.MESH)

    def hs(i):
        return slice(i * DH, (i + 1) * DH)

    loads = [
        pltpu.make_async_copy(src, dst, load_sems.at[n])
        for n, (src, dst) in enumerate((
            (dp_in, dp_ref), (tab_in, tab_ref), (op_in, op_ref), (k_in, k_ref),
            (v_in, v_ref), (q_in, q_ref), (ids_in, ids_ref), (cot_in, cot_ref),
        ))
    ]
    for load in loads:
        load.start()
    quarter = 2 * c + yl
    loads[0].wait()
    loads[1].wait()
    mine = c * 32
    qown = pl.ds(pl.multiple_of(quarter * 256, 256), 256)
    for a in range(3):
        rows8 = (dp_ref[:, qown] if a == 0 else tab_ref[a - 1, :, qown]).astype(F32)
        wz[3, a] = jnp.concatenate([rows8[:, :128], rows8[:, 128:]], axis=0).astype(BF16)
    loads[2].wait()
    pl.semaphore_wait(barrier, 10)

    own_p = op_ref.at[pl.ds(pl.multiple_of(mine, 32), 32), :]

    w_came, p_came, to_mate = {}, {}, {}

    def slot(rel):
        return (rel + 3) % nz

    def send_wz(rel, hop, device):
        w_came[rel - hop] = go.send(wz.at[slot(rel)], wz.at[slot(rel - hop)], device)

    def send_p(rel, hop, device):
        src = own_p if rel == 0 else proj.at[slot(rel), c]
        p_came[rel - hop] = go.send(src, proj.at[slot(rel - hop), c], device)

    def p_mate(rel):
        window = proj.at[slot(rel), c]
        to_mate[rel] = go.send(window, window, mate)

    around = ((1, zp), (-1, zm), (2, zp2), (-2, zm2))
    for hop, device in around:
        send_wz(0, hop, device)
    for hop, device in around:
        send_p(0, hop, device)
    for load in loads[3:]:
        load.wait()
    for i in range(4):
        s_own[i] = dot_tn(k_ref[:, hs(i)], v_ref[:, hs(i)]).astype(BF16)
    state_copy = go.send(s_own, s_recv, mate)
    proj[3] = op_ref[...].reshape(2, 32, 512)

    def relay_w(j):
        for sign, device in ((-1, zp2), (1, zm2)):
            for rel in (sign * (2 * j - 1), sign * 2 * j):
                w_came[rel].wait_recv()
                if rel != 6:
                    send_wz(rel, -2 * sign, device)

    def relay_p(j):
        for sign, device in ((-1, zp2), (1, zm2)):
            for rel in (sign * (2 * j - 1), sign * 2 * j):
                p_came[rel].wait_recv()
                if rel != 6:
                    send_p(rel, -2 * sign, device)
        for sign in (-1, 1):
            for rel in (sign * (2 * j - 1), sign * 2 * j):
                p_mate(rel)

    rows = lax.broadcasted_iota(jnp.int32, (HALF, HALF), 0)
    cols = lax.broadcasted_iota(jnp.int32, (HALF, HALF), 1)
    low = rows >= cols
    top, bot = slice(0, HALF), slice(HALF, 2 * HALF)

    def scores_of(a_ref, b_ref, i):
        a0, a1 = a_ref[top, hs(i)], a_ref[bot, hs(i)]
        b0, b1 = b_ref[top, hs(i)], b_ref[bot, hs(i)]
        m00 = jnp.where(low, dot_nt(a0, b0), 0.0).astype(BF16)
        m10 = dot_nt(a1, b0).astype(BF16)
        m11 = jnp.where(low, dot_nt(a1, b1), 0.0).astype(BF16)
        return m00, m10, m11

    def forward(i):
        m00, m10, m11 = scores_of(q_ref, k_ref, i)
        sc[i, 0], sc[i, 1], sc[i, 2] = m00, m10, m11
        v0, v1 = v_ref[top, hs(i)], v_ref[bot, hs(i)]
        acc[top, hs(i)] = dot(m00, v0)
        acc[bot, hs(i)] = dot(m10, v0) + dot(m11, v1)

    def pass_state():
        state_copy.wait_recv()
        t_own[...] = (s_own[...].astype(F32) + s_recv[...].astype(F32)).astype(BF16)
        return go.send(t_own, t_recv, pair)

    def finish_attended():
        pair_copy.wait_recv()
        s_in[...] = (cf * s_recv[...].astype(F32) + ylf * t_recv[...].astype(F32)).astype(BF16)
        for i in range(4):
            att[:, hs(i)] = (
                scale * (acc[:, hs(i)] + dot(q_ref[:, hs(i)], s_in[i]))
            ).astype(BF16)

    q0 = pl.multiple_of(quarter * 256, 256)
    ccols = pl.ds(pl.multiple_of(c * 512, 512), 512)

    def qcols(y_):
        return pl.ds(pl.multiple_of((2 * c + y_ % 2) * 256, 256), 256)

    def same(win, device):
        return go.send(win, win, device)

    w_mate = []

    class Plane:
        def __init__(self, group):
            self.g = group
            for a in range(3):
                block = wz[group * 8:group * 8 + 8, a].astype(F32)
                piece = jnp.concatenate(
                    [block[:, :8].reshape(64, 128), block[:, 8:].reshape(64, 128)], axis=1
                )
                wts[a, x, yh, group, :, pl.ds(q0, 256)] = piece.astype(BF16)
            self.wait_for = (
                same(self.ax(x, 0, 32), xp), same(self.ax(x, 0, 32), xm),
                same(self.by(y, 32, 32), yp), same(self.by(y, 32, 32), ym),
            )

        def ax(self, xx, r0, n):
            return wts.at[:, xx, yh, self.g, pl.ds(r0, n), qcols(y)]

        def by(self, yy, r0, n):
            return wts.at[:, x, yy // 2, self.g, pl.ds(r0, n), qcols(yy)]

        def ay(self, yy, r0, n):
            return wts.at[:, :, yy // 2, self.g, pl.ds(r0, n), qcols(yy)]

        def bx(self, xx, r0, n):
            return wts.at[:, xx, :, self.g, pl.ds(r0, n), ccols]

        def arrived(self):
            for copy in self.wait_for:
                copy.wait_recv()

        def second(self):
            self.arrived()
            self.wait_for = (
                same(self.ax(at_x(-1), 0, 16), xp), same(self.ax(at_x(1), 16, 16), xm),
                same(self.by(at_y(-1), 32, 16), yp), same(self.by(at_y(1), 48, 16), ym),
            )

        def third(self):
            self.arrived()
            self.wait_for = (
                same(self.ay(y, 0, 32), yp), same(self.ay(y, 0, 32), ym),
                same(self.bx(x, 32, 32), xp), same(self.bx(x, 32, 32), xm),
            )
            w_mate.append(same(self.ay(y, 0, 32), mate))
            w_mate.append(same(self.bx(x, 32, 32), mate))

        def fourth(self):
            self.arrived()
            self.wait_for = (
                same(self.ay(at_y(-1), 0, 16), yp), same(self.ay(at_y(1), 16, 16), ym),
                same(self.bx(at_x(-1), 32, 16), xp), same(self.bx(at_x(1), 48, 16), xm),
            )
            for step in (-1, 1):
                w_mate.append(same(self.ay(at_y(step), 0, 32), mate))
                w_mate.append(same(self.bx(at_x(step), 32, 32), mate))

        def fifth(self):
            self.arrived()
            w_mate.append(same(self.ay(at_y(2), 0, 32), mate))
            w_mate.append(same(self.bx(at_x(2), 32, 32), mate))

    class Reduce:
        def __init__(self, g, a0, b0, w):
            self.g, self.a0, self.b0, self.w = g, a0, b0, w
            self.c = pl.ds(0, w)
            self.block(b0)
            b = pl.ds(b0, w)
            self.y1 = (
                go.send(mix.at[:, 1 - yh, 0, :, b], rbr.at[g, 0, :, :, self.c], yp),
                go.send(mix.at[:, 1 - yh, 1, :, b], rbr.at[g, 1, :, :, self.c], ym),
            )
            self.block(a0)
            a = pl.ds(a0, w)
            self.x1 = (
                go.send(mix.at[at_x(2), 0, :, :, a], ra1.at[g, :, :, self.c], xp),
                go.send(mix.at[at_x(2), 1, :, :, a], rb1.at[g, :, :, self.c], xm),
            )

        def block(self, col):
            s0, n = col // 64, self.w // 64
            part = dot_nt(att[...], proj[s0:s0 + n].reshape(self.w, 512))
            mix[:, :, :, :, col:col + self.w] = part.astype(BF16).reshape(4, 2, 2, 32, self.w)

        def second(self):
            g, w, al = self.g, self.w, slice(self.a0, self.a0 + self.w)
            for copy in self.y1:
                copy.wait_recv()
            self.y2 = tuple(
                go.send(rbr.at[g, n, :, :, self.c], rbf.at[g, n, :, :, self.c], device)
                for n, device in ((0, yp), (1, ym))
            )
            for copy in self.x1:
                copy.wait_recv()
            mix[at_x(1), 0, :, :, al] = (
                mix[at_x(1), 0, :, :, al].astype(F32) + ra1[g, :, :, :w].astype(F32)
            ).astype(BF16)
            mix[at_x(-1), 1, :, :, al] = (
                mix[at_x(-1), 1, :, :, al].astype(F32) + rb1[g, :, :, :w].astype(F32)
            ).astype(BF16)
            a = pl.ds(self.a0, w)
            self.x2 = (
                go.send(mix.at[at_x(1), :, :, :, a], ra2.at[g, :, :, :, self.c], xp),
                go.send(mix.at[at_x(-1), :, :, :, a], rb2.at[g, :, :, :, self.c], xm),
            )

        def third(self):
            g, w = self.g, self.w
            al, be = slice(self.a0, self.a0 + w), slice(self.b0, self.b0 + w)
            for copy in self.y2:
                copy.wait_recv()
            for hf in range(2):
                yb[g, :, hf, :, :w] = (
                    mix[:, yh, hf, :, be].astype(F32) + rbf[g, hf, :, :, :w].astype(F32)
                ).astype(BF16)
            self.bx1 = tuple(
                go.send(yb.at[g, at_x(2), n, :, self.c], sb1.at[g, n, :, self.c], device)
                for n, device in ((0, xp), (1, xm))
            )
            for copy in self.x2:
                copy.wait_recv()
            ray[g, :, :, :w] = (
                mix[x, 1 - yh, :, :, al].astype(F32)
                + ra2[g, 1 - yh, :, :, :w].astype(F32)
                + rb2[g, 1 - yh, :, :, :w].astype(F32)
            ).astype(BF16)
            self.ay1 = tuple(
                go.send(ray.at[g, n, :, self.c], rar.at[g, n, :, self.c], device)
                for n, device in ((0, yp), (1, ym))
            )
            mixed[:, al] = (
                mix[x, yh, :, :, al].astype(F32)
                + ra2[g, yh, :, :, :w].astype(F32)
                + rb2[g, yh, :, :, :w].astype(F32)
            ).reshape(64, w)

        def fourth(self):
            g, w = self.g, self.w
            for copy in self.bx1:
                copy.wait_recv()
            for step, hf in ((1, 0), (-1, 1)):
                yb[g, at_x(step), hf, :, :w] = (
                    yb[g, at_x(step), hf, :, :w].astype(F32) + sb1[g, hf, :, :w].astype(F32)
                ).astype(BF16)
            self.bx2 = tuple(
                go.send(yb.at[g, at_x(step), :, :, self.c], sb2.at[g, n, :, :, self.c], device)
                for n, step, device in ((0, 1, xp), (1, -1, xm))
            )
            for copy in self.ay1:
                copy.wait_recv()
            self.ay2 = tuple(
                go.send(rar.at[g, n, :, self.c], raf.at[g, n, :, self.c], device)
                for n, device in ((0, yp), (1, ym))
            )

        def fifth(self):
            g, w = self.g, self.w
            al, be = slice(self.a0, self.a0 + w), slice(self.b0, self.b0 + w)
            for copy in self.ay2 + self.bx2:
                copy.wait_recv()
            mixed[:, al] = mixed[:, al] + raf[g, :, :, :w].astype(F32).reshape(64, w)
            mixed[:, be] = (
                yb[g, x, :, :, :w].astype(F32)
                + sb2[g, 0, :, :, :w].astype(F32)
                + sb2[g, 1, :, :, :w].astype(F32)
            ).reshape(64, w)

    forward(0)
    pair_copy = pass_state()
    forward(1)
    relay_w(1)
    relay_p(1)
    forward(2)
    forward(3)
    relay_w(2)
    near = Plane(0)
    relay_p(2)
    finish_attended()
    relay_w(3)
    near.second()
    for rel in (-1, -2, 1, 2, -3, 3, 4):
        to_mate[rel].wait_recv()
    mnear = Reduce(0, 0, 256, 256)
    relay_p(3)
    near.third()
    mnear.second()
    for rel in (-7, -8, 7):
        w_came[rel].wait_recv()
    far = Plane(1)
    for rel in (-7, -8, 7):
        p_came[rel].wait_recv()
        p_mate(rel)
    near.fourth()
    for rel in (-4, -5, -6, 5, 6, -7, -8, 7):
        to_mate[rel].wait_recv()
    mfar = Reduce(1, 512, 768, 256)
    mnear.third()
    far.second()
    mfar.second()
    far.third()
    mnear.fourth()
    near.fifth()
    mfar.third()
    mnear.fifth()
    mfar.fourth()
    far.fourth()
    mfar.fifth()
    far.fifth()
    for copy in w_mate:
        copy.wait_recv()

    def weight(a, xx):
        return wts[a, xx].reshape(256, 1024)

    turn = (z * 8 + 128 - 24) % 128
    place = lax.broadcasted_iota(jnp.int32, (256, 64), 0)
    vocab = place - place % 128 + (place % 128 + turn) % 128
    for level in range(2):
        ids = ids_ref[level:level + 1, :]
        total = None
        for xx in range(4):
            onehot = jnp.where(ids - 256 * xx == vocab, 1.0, 0.0).astype(BF16)
            term = dot_tn(onehot, weight(1 + level, xx))
            total = term if total is None else total + term
        emb[level] = total

    def turned(value, by):
        return jnp.concatenate(
            [pltpu.roll(value[:, 128 * j:128 * j + 128], by, 1) for j in range(8)], axis=1
        )

    def back_through(g):
        g = turned(g, (128 - turn) % 128).astype(BF16)
        total = None
        for xx in range(4):
            term = dot(g[:, 256 * xx:256 * xx + 256], weight(0, xx))
            total = term if total is None else total + term
        return total

    gpre[...] = back_through(cot_ref[:, 1, :].astype(F32))

    def mean_of(value):
        return jnp.mean(value, axis=-1, keepdims=True)

    shift = (z * 64 + 1024 - 192) % 1024
    summed1 = pltpu.roll(mixed[...], shift, 1) + emb[0]
    r1 = lax.rsqrt(mean_of(summed1 * summed1) + EPS)
    normed1 = (summed1 * r1).astype(BF16)
    mixed[...] = summed1
    proj1 = turned(
        jnp.concatenate([dot_nt(normed1, weight(0, xx)) for xx in range(4)], axis=1), turn
    )
    sig = jax.nn.sigmoid(proj1)
    summed2 = summed1 + proj1 * sig + emb[1]
    r2 = lax.rsqrt(mean_of(summed2 * summed2) + EPS)
    g2 = gpre[...]
    gsum = r2 * g2 - summed2 * (r2 * r2 * r2 * mean_of(g2 * summed2))
    emb[0] = gsum
    gproj = cot_ref[:, 0, :].astype(F32) + gsum * (sig * (1.0 + proj1 * (1.0 - sig)))
    g1 = back_through(gproj)
    summed1 = mixed[...]
    grad = emb[0] + r1 * g1 - summed1 * (r1 * r1 * r1 * mean_of(g1 * summed1))
    grad = pltpu.roll(grad, (1024 - shift) % 1024, 1)
    gb[x, yh] = grad.astype(BF16).reshape(2, 32, 1024)

    class Spread:
        def __init__(self, group, a0, b0, w):
            self.a, self.b = pl.ds(a0, w), pl.ds(b0, w)
            self.ra, self.rb = gra.at[group, :, :, :, pl.ds(0, w)], grb.at[group, :, :, pl.ds(0, w)]
            self.y1 = (
                go.send(gb.at[x, yh, 0, :, self.b], self.rb.at[0], yp),
                go.send(gb.at[x, yh, 1, :, self.b], self.rb.at[1], ym),
            )
            own = gb.at[x, yh, :, :, self.a]
            self.x1 = (same(own, xp), same(own, xm))

        def second(self):
            for copy in self.y1:
                copy.wait_recv()
            self.y2 = (
                go.send(self.rb.at[0], gb.at[x, at_y(-1) // 2, 0, :, self.b], yp),
                go.send(self.rb.at[1], gb.at[x, at_y(1) // 2, 1, :, self.b], ym),
            )
            for copy in self.x1:
                copy.wait_recv()
            self.x2 = (
                same(gb.at[at_x(-1), yh, 0, :, self.a], xp),
                same(gb.at[at_x(1), yh, 1, :, self.a], xm),
            )

        def third(self):
            for copy in self.y2:
                copy.wait_recv()
            own = gb.at[x, :, :, :, self.b]
            self.bx1 = (same(own, xp), same(own, xm))
            for copy in self.x2:
                copy.wait_recv()
            self.ay1 = (
                go.send(gb.at[:, yh, 0, :, self.a], self.ra.at[0], yp),
                go.send(gb.at[:, yh, 1, :, self.a], self.ra.at[1], ym),
            )

        def fourth(self):
            for copy in self.bx1:
                copy.wait_recv()
            self.bx2 = (
                same(gb.at[at_x(-1), 0, :, :, self.b], xp),
                same(gb.at[at_x(1), 1, :, :, self.b], xm),
            )
            for copy in self.ay1:
                copy.wait_recv()
            self.ay2 = (
                go.send(self.ra.at[0], gb.at[:, at_y(-1) // 2, 0, :, self.a], yp),
                go.send(self.ra.at[1], gb.at[:, at_y(1) // 2, 1, :, self.a], ym),
            )

        def fifth(self):
            for copy in self.bx2 + self.ay2:
                copy.wait_recv()

    def weight_grad(s0, n):
        block = gb[:, :, :, :, 64 * s0:64 * (s0 + n)].reshape(512, 64 * n)
        wg[s0:s0 + n] = dot_tn(block, att[...]).astype(BF16).reshape(n, 2, 32, 512)
        rows_n = pl.ds(s0, n)
        return go.send(wg.at[rows_n, 1 - c], wgr.at[rows_n], mate)

    def own_chunk(rel):
        return wg[slot(rel), c].astype(F32) + wgr[slot(rel)].astype(F32)

    chains = ((8, 4), (7, 4), (-7, 4), (-6, 3))
    came = [None] * 4

    def chain_step(m):
        for n, (first, length) in enumerate(chains):
            if m >= length:
                continue
            sign = 1 if first > 0 else -1
            dist = first - 2 * sign * m
            value = own_chunk(dist)
            if m > 0:
                came[n].wait_recv()
                value = value + zrecv[n, m - 1].astype(F32)
            zsend[n, m] = value.astype(BF16)
            device = {2: zp2, 1: zp, -1: zm, -2: zm2}[max(-2, min(2, dist))]
            came[n] = go.send(zsend.at[n, m], zrecv.at[n, m], device)

    spread_far = Spread(2, 640, 768, 128)
    spread_mid = Spread(1, 512, 896, 128)
    spread_far.second()
    spread_mid.second()
    spread_far.third()
    spread_mid.third()
    spread_near = Spread(0, 0, 256, 256)
    spread_far.fourth()
    spread_mid.fourth()
    spread_near.second()
    spread_far.fifth()
    wg_far = weight_grad(10, 4)
    spread_mid.fifth()
    wg_mid = (weight_grad(8, 2), weight_grad(14, 2))
    spread_near.third()
    wg_far.wait_recv()
    chain_step(0)
    spread_near.fourth()
    for copy in wg_mid:
        copy.wait_recv()
    chain_step(1)
    spread_near.fifth()
    wg_near = (weight_grad(0, 4), weight_grad(4, 4))

    for j in range(2):
        total = None
        for zz in range(4):
            term = dot(
                gb[:, :, :, :, 256 * zz:256 * zz + 256].reshape(512, 256),
                proj[4 * zz:4 * zz + 4, :, :, 256 * j:256 * j + 256].reshape(256, 256),
            )
            total = term if total is None else total + term
        ga[:, 256 * j:256 * j + 256] = total.astype(BF16)

    for i in range(4):
        b_own[i] = dot_tn(q_ref[:, hs(i)], ga[:, hs(i)]).astype(BF16)
    back_copy = go.send(b_own, b_recv, mate)

    def backward(i):
        q0_, q1_ = q_ref[top, hs(i)], q_ref[bot, hs(i)]
        k0_, k1_ = k_ref[top, hs(i)], k_ref[bot, hs(i)]
        v0_, v1_ = v_ref[top, hs(i)], v_ref[bot, hs(i)]
        a0_, a1_ = ga[top, hs(i)], ga[bot, hs(i)]
        m00, m10, m11 = scores_of(ga, v_ref, i)
        e, b = s_in[i], b_in[i]
        gq_ref[top, hs(i)] = (scale * (dot(m00, k0_) + dot_nt(a0_, e))).astype(BF16)
        gq_ref[bot, hs(i)] = (
            scale * (dot(m10, k0_) + dot(m11, k1_) + dot_nt(a1_, e))
        ).astype(BF16)
        gk_ref[top, hs(i)] = (
            scale * (dot_tn(m00, q0_) + dot_tn(m10, q1_) + dot_nt(v0_, b))
        ).astype(BF16)
        gk_ref[bot, hs(i)] = (scale * (dot_tn(m11, q1_) + dot_nt(v1_, b))).astype(BF16)
        gv_ref[top, hs(i)] = (
            scale * (dot_tn(sc[i, 0], a0_) + dot_tn(sc[i, 1], a1_) + dot(k0_, b))
        ).astype(BF16)
        gv_ref[bot, hs(i)] = (scale * (dot_tn(sc[i, 2], a1_) + dot(k1_, b))).astype(BF16)

    back_copy.wait_recv()
    bt_own[...] = (b_own[...].astype(F32) + b_recv[...].astype(F32)).astype(BF16)
    back_pair = go.send(bt_own, bt_recv, pair)
    for copy in wg_near:
        copy.wait_recv()
    chain_step(2)
    chain_step(3)
    back_pair.wait_recv()
    b_in[...] = (
        (1.0 - cf) * b_recv[...].astype(F32) + (1.0 - ylf) * bt_recv[...].astype(F32)
    ).astype(BF16)
    backward(0)
    backward(1)
    total = own_chunk(0)
    for n, (first, length) in enumerate(chains):
        came[n].wait_recv()
        total = total + zrecv[n, length - 1].astype(F32)
    y_own[...] = total.astype(BF16)
    last = [go.send(y_own, y_recv.at[n], device) for n, device in enumerate((pair, mate, cross))]
    backward(2)
    backward(3)
    for copy in last:
        copy.wait_recv()
    go_ref[pl.ds(pl.multiple_of(mine, 32), 32), :] = (
        y_own[...].astype(F32) + y_recv[0].astype(F32)
    )
    go_ref[pl.ds(pl.multiple_of(32 - mine, 32), 32), :] = (
        y_recv[1].astype(F32) + y_recv[2].astype(F32)
    )
    go.drain()


def out_kernel(*refs):
    copies = [
        pltpu.make_async_copy(refs[n], refs[4 + n], refs[8].at[n]) for n in range(4)
    ]
    for copy in copies:
        copy.start()
    for copy in copies:
        copy.wait()


def write_out(*arrays):
    return pl.pallas_call(
        out_kernel,
        out_shape=tuple(jax.ShapeDtypeStruct(a.shape, a.dtype) for a in arrays),
        in_specs=[pl.BlockSpec(memory_space=pltpu.VMEM)] * 4,
        out_specs=(pl.BlockSpec(memory_space=pltpu.HBM),) * 4,
        scratch_shapes=[pltpu.SemaphoreType.DMA((4,))],
        compiler_params=pltpu.CompilerParams(vmem_limit_bytes=8 * 1024 * 1024),
        name="write_out",
    )(*arrays)


def on_device(queries, keys, values, out_proj, depth_proj, code_table, code_ids, depth_cotangent):
    scale = 2048.0 ** (-0.5)
    def vm(shape, kind=BF16):
        return pltpu.VMEM(shape, kind)

    state = vm((4, DH, DH))
    gq, gk, gv, gop = pl.pallas_call(
        functools.partial(kernel, scale),
        out_shape=(
            jax.ShapeDtypeStruct((512, 512), BF16),
            jax.ShapeDtypeStruct((512, 512), BF16),
            jax.ShapeDtypeStruct((512, 512), BF16),
            jax.ShapeDtypeStruct((64, 512), F32),
        ),
        in_specs=[pl.BlockSpec(memory_space=pltpu.HBM)] * 8,
        out_specs=(pl.BlockSpec(memory_space=pltpu.VMEM),) * 4,
        scratch_shapes=[
            vm((512, 512)), vm((512, 512)), vm((512, 512)), vm((64, 512)),
            vm((8, 1024)), vm((2, 8, 1024)), vm((2, 64), jnp.int32), vm((64, 2, 1024)),
            pltpu.SemaphoreType.DMA((8,)),
            vm((16, 3, 16, 128)), vm((16, 2, 32, 512)), vm((3, 4, 2, 2, 64, 1024)),
            state, state, state, state, state,
            state, state, state, state, state,
            vm((4, 3, 256, 256)), vm((512, 512), F32), vm((512, 512)),
            vm((4, 2, 2, 32, 1024)),
            vm((3, 2, 32, 256)), vm((3, 2, 32, 256)),
            vm((3, 2, 2, 32, 256)), vm((3, 2, 2, 32, 256)),
            vm((3, 2, 32, 256)), vm((3, 2, 32, 256)), vm((3, 2, 32, 256)),
            vm((3, 2, 4, 32, 256)), vm((3, 2, 4, 32, 256)),
            vm((3, 4, 2, 32, 256)), vm((3, 2, 32, 256)), vm((3, 2, 2, 32, 256)),
            vm((64, 1024), F32), vm((2, 64, 1024), F32), vm((64, 1024), F32),
            vm((4, 2, 2, 32, 1024)), vm((3, 2, 4, 32, 256)), vm((3, 2, 32, 256)),
            vm((512, 512)), vm((16, 2, 32, 512)), vm((16, 32, 512)),
            vm((4, 4, 32, 512)), vm((4, 4, 32, 512)),
            vm((32, 512)), vm((3, 32, 512)),
            pltpu.SemaphoreType.DMA((N_COPIES,)),
            pltpu.SemaphoreType.DMA((N_COPIES,)),
        ],
        compiler_params=pltpu.CompilerParams(
            collective_id=0, has_side_effects=True, vmem_limit_bytes=34 * 1024 * 1024
        ),
        name="fused_step",
    )(
        *(
            pltpu.with_memory_space_constraint(array, pltpu.HBM)
            for array in (
                queries[0], keys[0], values[0], out_proj.T, depth_proj.T, code_table,
                code_ids[0].T, depth_cotangent[0],
            )
        )
    )
    gq, gk, gv, gop = write_out(gq, gk, gv, gop)
    return gq[None], gk[None], gv[None], gop.T


def solution(mesh):
    in_specs = (
        P("dp", "seq", "head"),
        P("dp", "seq", "head"),
        P("dp", "seq", "head"),
        P("head", "dp"),
        P(None, ("head", "dp")),
        P(None, ("head", "dp"), None),
        P("dp", ("seq", "head"), None),
        P("dp", ("seq", "head"), None, None),
    )
    out_specs = (
        P("dp", "seq", "head"),
        P("dp", "seq", "head"),
        P("dp", "seq", "head"),
        P("head", "dp"),
    )
    return jax.shard_map(
        on_device, mesh=mesh, in_specs=in_specs, out_specs=out_specs, check_vma=False
    )
```

```python
import functools

import jax
import jax.numpy as jnp
from jax import lax
from jax.experimental import pallas as pl
from jax.experimental.pallas import tpu as pltpu
from jax.sharding import PartitionSpec as P

DH = 128
F32 = jnp.float32
BF16 = jnp.bfloat16
EPS = 1e-05
HALF = 256
N_COPIES = 256


def dot(a, b):
    return lax.dot_general(a, b, (((1,), (0,)), ((), ())), preferred_element_type=F32)


def dot_nt(a, b):
    return lax.dot_general(a, b, (((1,), (1,)), ((), ())), preferred_element_type=F32)


def dot_tn(a, b):
    return lax.dot_general(a, b, (((0,), (0,)), ((), ())), preferred_element_type=F32)


class Copies:
    def __init__(self, send_sems, recv_sems):
        self.send_sems, self.recv_sems, self.all = send_sems, recv_sems, []

    def send(self, src, dst, device):
        index = len(self.all)
        copy = pltpu.make_async_remote_copy(
            src_ref=src,
            dst_ref=dst,
            send_sem=self.send_sems.at[index],
            recv_sem=self.recv_sems.at[index],
            device_id=device,
            device_id_type=pl.DeviceIdType.MESH,
        )
        copy.start()
        self.all.append(copy)
        return copy

    def drain(self):
        for copy in self.all:
            copy.wait_send()


def kernel(
    scale,
    q_in, k_in, v_in, op_in, dp_in, tab_in, ids_in, cot_in,
    gq_ref, gk_ref, gv_ref, go_ref,
    q_ref, k_ref, v_ref, op_ref, dp_ref, tab_ref, ids_ref, cot_ref, load_sems,
    wz, proj, wts,
    s_own, s_recv, t_own, t_recv, s_in,
    b_own, b_recv, bt_own, bt_recv, b_in,
    sc, acc, att,
    mix, ra1, rb1, ra2, rb2, ray, rar, raf, rbr, rbf, yb, sb1, sb2,
    mixed, emb, gpre,
    gb, gra, grb,
    ga, wg, wgr, zsend, zrecv, y_own, y_recv,
    send_sems, recv_sems,
):
    seq, head, z = lax.axis_index("seq"), lax.axis_index("head"), lax.axis_index("dp")
    x, yh, yl, c = head // 2, head % 2, seq // 2, seq % 2
    y = 2 * yh + yl
    nz = 16

    def at_x(step):
        return (x + step + 4) % 4

    def at_y(step):
        return (y + step + 4) % 4

    def at_z(step):
        return (z + step + nz) % nz

    def dev(x_=None, y_=None, z_=None, c_=None):
        x_ = x if x_ is None else x_
        y_ = y if y_ is None else y_
        z_ = z if z_ is None else z_
        c_ = c if c_ is None else c_
        return {"seq": 2 * (y_ % 2) + c_, "head": 2 * x_ + y_ // 2, "dp": z_}

    xp, xm = dev(x_=at_x(1)), dev(x_=at_x(-1))
    yp, ym = dev(y_=at_y(1)), dev(y_=at_y(-1))
    zp, zm = dev(z_=at_z(1)), dev(z_=at_z(-1))
    zp2, zm2 = dev(z_=at_z(2)), dev(z_=at_z(-2))
    mate = dev(c_=1 - c)
    pair = dev(y_=2 * yh + 1 - yl)
    cross = dev(y_=2 * yh + 1 - yl, c_=1 - c)
    cf, ylf = c.astype(F32), yl.astype(F32)
    go = Copies(send_sems, recv_sems)

    barrier = pltpu.get_barrier_semaphore()
    for other in (xp, xm, yp, ym, zp, zm, zp2, zm2, mate, cross):
        pl.semaphore_signal(barrier, inc=1, device_id=other, device_id_type=pl.DeviceIdType.MESH)

    def hs(i):
        return slice(i * DH, (i + 1) * DH)

    loads = [
        pltpu.make_async_copy(src, dst, load_sems.at[n])
        for n, (src, dst) in enumerate((
            (dp_in, dp_ref), (tab_in, tab_ref), (op_in, op_ref), (k_in, k_ref),
            (v_in, v_ref), (q_in, q_ref), (ids_in, ids_ref), (cot_in, cot_ref),
        ))
    ]
    for load in loads:
        load.start()
    quarter = 2 * c + yl
    loads[0].wait()
    loads[1].wait()
    mine = c * 32
    qown = pl.ds(pl.multiple_of(quarter * 256, 256), 256)
    for a in range(3):
        rows8 = (dp_ref[:, qown] if a == 0 else tab_ref[a - 1, :, qown]).astype(F32)
        wz[3, a] = jnp.concatenate([rows8[:, :128], rows8[:, 128:]], axis=0).astype(BF16)
    loads[2].wait()
    pl.semaphore_wait(barrier, 10)

    own_p = op_ref.at[pl.ds(pl.multiple_of(mine, 32), 32), :]

    w_came, p_came, to_mate = {}, {}, {}

    def slot(rel):
        return (rel + 3) % nz

    def send_wz(rel, hop, device):
        w_came[rel - hop] = go.send(wz.at[slot(rel)], wz.at[slot(rel - hop)], device)

    def send_p(rel, hop, device):
        src = own_p if rel == 0 else proj.at[slot(rel), c]
        p_came[rel - hop] = go.send(src, proj.at[slot(rel - hop), c], device)

    def p_mate(rel):
        window = proj.at[slot(rel), c]
        to_mate[rel] = go.send(window, window, mate)

    around = ((1, zp), (-1, zm), (2, zp2), (-2, zm2))
    for hop, device in around:
        send_wz(0, hop, device)
    for hop, device in around:
        send_p(0, hop, device)
    for load in loads[3:]:
        load.wait()
    for i in range(4):
        s_own[i] = dot_tn(k_ref[:, hs(i)], v_ref[:, hs(i)]).astype(BF16)
    state_copy = go.send(s_own, s_recv, mate)
    proj[3] = op_ref[...].reshape(2, 32, 512)

    def relay_w(j):
        for sign, device in ((-1, zp2), (1, zm2)):
            for rel in (sign * (2 * j - 1), sign * 2 * j):
                w_came[rel].wait_recv()
                if rel != 6:
                    send_wz(rel, -2 * sign, device)

    def relay_p(j):
        for sign, device in ((-1, zp2), (1, zm2)):
            for rel in (sign * (2 * j - 1), sign * 2 * j):
                p_came[rel].wait_recv()
                if rel != 6:
                    send_p(rel, -2 * sign, device)
        for sign in (-1, 1):
            for rel in (sign * (2 * j - 1), sign * 2 * j):
                p_mate(rel)

    rows = lax.broadcasted_iota(jnp.int32, (HALF, HALF), 0)
    cols = lax.broadcasted_iota(jnp.int32, (HALF, HALF), 1)
    low = rows >= cols
    top, bot = slice(0, HALF), slice(HALF, 2 * HALF)

    def scores_of(a_ref, b_ref, i):
        a0, a1 = a_ref[top, hs(i)], a_ref[bot, hs(i)]
        b0, b1 = b_ref[top, hs(i)], b_ref[bot, hs(i)]
        m00 = jnp.where(low, dot_nt(a0, b0), 0.0).astype(BF16)
        m10 = dot_nt(a1, b0).astype(BF16)
        m11 = jnp.where(low, dot_nt(a1, b1), 0.0).astype(BF16)
        return m00, m10, m11

    def forward(i):
        m00, m10, m11 = scores_of(q_ref, k_ref, i)
        sc[i, 0], sc[i, 1], sc[i, 2] = m00, m10, m11
        v0, v1 = v_ref[top, hs(i)], v_ref[bot, hs(i)]
        acc[top, hs(i)] = dot(m00, v0)
        acc[bot, hs(i)] = dot(m10, v0) + dot(m11, v1)

    def pass_state():
        state_copy.wait_recv()
        t_own[...] = (s_own[...].astype(F32) + s_recv[...].astype(F32)).astype(BF16)
        return go.send(t_own, t_recv, pair)

    def finish_attended():
        pair_copy.wait_recv()
        s_in[...] = (cf * s_recv[...].astype(F32) + ylf * t_recv[...].astype(F32)).astype(BF16)
        for i in range(4):
            att[:, hs(i)] = (
                scale * (acc[:, hs(i)] + dot(q_ref[:, hs(i)], s_in[i]))
            ).astype(BF16)

    q0 = pl.multiple_of(quarter * 256, 256)
    ccols = pl.ds(pl.multiple_of(c * 512, 512), 512)

    def qcols(y_):
        return pl.ds(pl.multiple_of((2 * c + y_ % 2) * 256, 256), 256)

    def same(win, device):
        return go.send(win, win, device)

    w_mate = []

    class Plane:
        def __init__(self, group):
            self.g = group
            for a in range(3):
                block = wz[group * 8:group * 8 + 8, a].astype(F32)
                piece = jnp.concatenate(
                    [block[:, :8].reshape(64, 128), block[:, 8:].reshape(64, 128)], axis=1
                )
                wts[a, x, yh, group, :, pl.ds(q0, 256)] = piece.astype(BF16)
            self.wait_for = (
                same(self.ax(x, 0, 32), xp), same(self.ax(x, 0, 32), xm),
                same(self.by(y, 32, 32), yp), same(self.by(y, 32, 32), ym),
            )

        def ax(self, xx, r0, n):
            return wts.at[:, xx, yh, self.g, pl.ds(r0, n), qcols(y)]

        def by(self, yy, r0, n):
            return wts.at[:, x, yy // 2, self.g, pl.ds(r0, n), qcols(yy)]

        def ay(self, yy, r0, n):
            return wts.at[:, :, yy // 2, self.g, pl.ds(r0, n), qcols(yy)]

        def bx(self, xx, r0, n):
            return wts.at[:, xx, :, self.g, pl.ds(r0, n), ccols]

        def arrived(self):
            for copy in self.wait_for:
                copy.wait_recv()

        def second(self):
            self.arrived()
            self.wait_for = (
                same(self.ax(at_x(-1), 0, 16), xp), same(self.ax(at_x(1), 16, 16), xm),
                same(self.by(at_y(-1), 32, 16), yp), same(self.by(at_y(1), 48, 16), ym),
            )

        def third(self):
            self.arrived()
            self.wait_for = (
                same(self.ay(y, 0, 32), yp), same(self.ay(y, 0, 32), ym),
                same(self.bx(x, 32, 32), xp), same(self.bx(x, 32, 32), xm),
            )
            w_mate.append(same(self.ay(y, 0, 32), mate))
            w_mate.append(same(self.bx(x, 32, 32), mate))

        def fourth(self):
            self.arrived()
            self.wait_for = (
                same(self.ay(at_y(-1), 0, 16), yp), same(self.ay(at_y(1), 16, 16), ym),
                same(self.bx(at_x(-1), 32, 16), xp), same(self.bx(at_x(1), 48, 16), xm),
            )
            for step in (-1, 1):
                w_mate.append(same(self.ay(at_y(step), 0, 32), mate))
                w_mate.append(same(self.bx(at_x(step), 32, 32), mate))

        def fifth(self):
            self.arrived()
            w_mate.append(same(self.ay(at_y(2), 0, 32), mate))
            w_mate.append(same(self.bx(at_x(2), 32, 32), mate))

    class Reduce:
        def __init__(self, g, a0, b0, w):
            self.g, self.a0, self.b0, self.w = g, a0, b0, w
            self.c = pl.ds(0, w)
            self.block(b0)
            b = pl.ds(b0, w)
            self.y1 = (
                go.send(mix.at[:, 1 - yh, 0, :, b], rbr.at[g, 0, :, :, self.c], yp),
                go.send(mix.at[:, 1 - yh, 1, :, b], rbr.at[g, 1, :, :, self.c], ym),
            )
            self.block(a0)
            a = pl.ds(a0, w)
            self.x1 = (
                go.send(mix.at[at_x(2), 0, :, :, a], ra1.at[g, :, :, self.c], xp),
                go.send(mix.at[at_x(2), 1, :, :, a], rb1.at[g, :, :, self.c], xm),
            )

        def block(self, col):
            s0, n = col // 64, self.w // 64
            part = dot_nt(att[...], proj[s0:s0 + n].reshape(self.w, 512))
            mix[:, :, :, :, col:col + self.w] = part.astype(BF16).reshape(4, 2, 2, 32, self.w)

        def second(self):
            g, w, al = self.g, self.w, slice(self.a0, self.a0 + self.w)
            for copy in self.y1:
                copy.wait_recv()
            self.y2 = tuple(
                go.send(rbr.at[g, n, :, :, self.c], rbf.at[g, n, :, :, self.c], device)
                for n, device in ((0, yp), (1, ym))
            )
            for copy in self.x1:
                copy.wait_recv()
            mix[at_x(1), 0, :, :, al] = (
                mix[at_x(1), 0, :, :, al].astype(F32) + ra1[g, :, :, :w].astype(F32)
            ).astype(BF16)
            mix[at_x(-1), 1, :, :, al] = (
                mix[at_x(-1), 1, :, :, al].astype(F32) + rb1[g, :, :, :w].astype(F32)
            ).astype(BF16)
            a = pl.ds(self.a0, w)
            self.x2 = (
                go.send(mix.at[at_x(1), :, :, :, a], ra2.at[g, :, :, :, self.c], xp),
                go.send(mix.at[at_x(-1), :, :, :, a], rb2.at[g, :, :, :, self.c], xm),
            )

        def third(self):
            g, w = self.g, self.w
            al, be = slice(self.a0, self.a0 + w), slice(self.b0, self.b0 + w)
            for copy in self.y2:
                copy.wait_recv()
            for hf in range(2):
                yb[g, :, hf, :, :w] = (
                    mix[:, yh, hf, :, be].astype(F32) + rbf[g, hf, :, :, :w].astype(F32)
                ).astype(BF16)
            self.bx1 = tuple(
                go.send(yb.at[g, at_x(2), n, :, self.c], sb1.at[g, n, :, self.c], device)
                for n, device in ((0, xp), (1, xm))
            )
            for copy in self.x2:
                copy.wait_recv()
            ray[g, :, :, :w] = (
                mix[x, 1 - yh, :, :, al].astype(F32)
                + ra2[g, 1 - yh, :, :, :w].astype(F32)
                + rb2[g, 1 - yh, :, :, :w].astype(F32)
            ).astype(BF16)
            self.ay1 = tuple(
                go.send(ray.at[g, n, :, self.c], rar.at[g, n, :, self.c], device)
                for n, device in ((0, yp), (1, ym))
            )
            mixed[:, al] = (
                mix[x, yh, :, :, al].astype(F32)
                + ra2[g, yh, :, :, :w].astype(F32)
                + rb2[g, yh, :, :, :w].astype(F32)
            ).reshape(64, w)

        def fourth(self):
            g, w = self.g, self.w
            for copy in self.bx1:
                copy.wait_recv()
            for step, hf in ((1, 0), (-1, 1)):
                yb[g, at_x(step), hf, :, :w] = (
                    yb[g, at_x(step), hf, :, :w].astype(F32) + sb1[g, hf, :, :w].astype(F32)
                ).astype(BF16)
            self.bx2 = tuple(
                go.send(yb.at[g, at_x(step), :, :, self.c], sb2.at[g, n, :, :, self.c], device)
                for n, step, device in ((0, 1, xp), (1, -1, xm))
            )
            for copy in self.ay1:
                copy.wait_recv()
            self.ay2 = tuple(
                go.send(rar.at[g, n, :, self.c], raf.at[g, n, :, self.c], device)
                for n, device in ((0, yp), (1, ym))
            )

        def fifth(self):
            g, w = self.g, self.w
            al, be = slice(self.a0, self.a0 + w), slice(self.b0, self.b0 + w)
            for copy in self.ay2 + self.bx2:
                copy.wait_recv()
            mixed[:, al] = mixed[:, al] + raf[g, :, :, :w].astype(F32).reshape(64, w)
            mixed[:, be] = (
                yb[g, x, :, :, :w].astype(F32)
                + sb2[g, 0, :, :, :w].astype(F32)
                + sb2[g, 1, :, :, :w].astype(F32)
            ).reshape(64, w)

    forward(0)
    pair_copy = pass_state()
    forward(1)
    relay_w(1)
    relay_p(1)
    forward(2)
    forward(3)
    relay_w(2)
    near = Plane(0)
    relay_p(2)
    finish_attended()
    relay_w(3)
    near.second()
    for rel in (-1, -2, 1, 2, -3, 3, 4):
        to_mate[rel].wait_recv()
    mnear = Reduce(0, 0, 256, 256)
    relay_p(3)
    for rel in (-7, -8, 7):
        w_came[rel].wait_recv()
    far = Plane(1)
    near.third()
    mnear.second()
    for rel in (-7, -8, 7):
        p_came[rel].wait_recv()
        p_mate(rel)
    far.second()
    near.fourth()
    for rel in (-4, -5, -6, 5, 6, -7, -8, 7):
        to_mate[rel].wait_recv()
    mfar = Reduce(1, 512, 768, 256)
    far.third()
    mnear.third()
    mfar.second()
    mnear.fourth()
    near.fifth()
    mfar.third()
    far.fourth()
    mnear.fifth()
    mfar.fourth()
    mfar.fifth()
    far.fifth()
    for copy in w_mate:
        copy.wait_recv()

    def weight(a, xx):
        return wts[a, xx].reshape(256, 1024)

    turn = (z * 8 + 128 - 24) % 128
    place = lax.broadcasted_iota(jnp.int32, (256, 64), 0)
    vocab = place - place % 128 + (place % 128 + turn) % 128
    for level in range(2):
        ids = ids_ref[level:level + 1, :]
        total = None
        for xx in range(4):
            onehot = jnp.where(ids - 256 * xx == vocab, 1.0, 0.0).astype(BF16)
            term = dot_tn(onehot, weight(1 + level, xx))
            total = term if total is None else total + term
        emb[level] = total

    def turned(value, by):
        return jnp.concatenate(
            [pltpu.roll(value[:, 128 * j:128 * j + 128], by, 1) for j in range(8)], axis=1
        )

    def back_through(g):
        g = turned(g, (128 - turn) % 128).astype(BF16)
        total = None
        for xx in range(4):
            term = dot(g[:, 256 * xx:256 * xx + 256], weight(0, xx))
            total = term if total is None else total + term
        return total

    gpre[...] = back_through(cot_ref[:, 1, :].astype(F32))

    def mean_of(value):
        return jnp.mean(value, axis=-1, keepdims=True)

    shift = (z * 64 + 1024 - 192) % 1024
    summed1 = pltpu.roll(mixed[...], shift, 1) + emb[0]
    r1 = lax.rsqrt(mean_of(summed1 * summed1) + EPS)
    normed1 = (summed1 * r1).astype(BF16)
    mixed[...] = summed1
    proj1 = turned(
        jnp.concatenate([dot_nt(normed1, weight(0, xx)) for xx in range(4)], axis=1), turn
    )
    sig = jax.nn.sigmoid(proj1)
    summed2 = summed1 + proj1 * sig + emb[1]
    r2 = lax.rsqrt(mean_of(summed2 * summed2) + EPS)
    g2 = gpre[...]
    gsum = r2 * g2 - summed2 * (r2 * r2 * r2 * mean_of(g2 * summed2))
    emb[0] = gsum
    gproj = cot_ref[:, 0, :].astype(F32) + gsum * (sig * (1.0 + proj1 * (1.0 - sig)))
    g1 = back_through(gproj)
    summed1 = mixed[...]
    grad = emb[0] + r1 * g1 - summed1 * (r1 * r1 * r1 * mean_of(g1 * summed1))
    grad = pltpu.roll(grad, (1024 - shift) % 1024, 1)
    gb[x, yh] = grad.astype(BF16).reshape(2, 32, 1024)

    class Spread:
        def __init__(self, group, a0, b0, w):
            self.a, self.b = pl.ds(a0, w), pl.ds(b0, w)
            self.ra, self.rb = gra.at[group, :, :, :, pl.ds(0, w)], grb.at[group, :, :, pl.ds(0, w)]
            self.y1 = (
                go.send(gb.at[x, yh, 0, :, self.b], self.rb.at[0], yp),
                go.send(gb.at[x, yh, 1, :, self.b], self.rb.at[1], ym),
            )
            own = gb.at[x, yh, :, :, self.a]
            self.x1 = (same(own, xp), same(own, xm))

        def second(self):
            for copy in self.y1:
                copy.wait_recv()
            self.y2 = (
                go.send(self.rb.at[0], gb.at[x, at_y(-1) // 2, 0, :, self.b], yp),
                go.send(self.rb.at[1], gb.at[x, at_y(1) // 2, 1, :, self.b], ym),
            )
            for copy in self.x1:
                copy.wait_recv()
            self.x2 = (
                same(gb.at[at_x(-1), yh, 0, :, self.a], xp),
                same(gb.at[at_x(1), yh, 1, :, self.a], xm),
            )

        def third(self):
            for copy in self.y2:
                copy.wait_recv()
            own = gb.at[x, :, :, :, self.b]
            self.bx1 = (same(own, xp), same(own, xm))
            for copy in self.x2:
                copy.wait_recv()
            self.ay1 = (
                go.send(gb.at[:, yh, 0, :, self.a], self.ra.at[0], yp),
                go.send(gb.at[:, yh, 1, :, self.a], self.ra.at[1], ym),
            )

        def fourth(self):
            for copy in self.bx1:
                copy.wait_recv()
            self.bx2 = (
                same(gb.at[at_x(-1), 0, :, :, self.b], xp),
                same(gb.at[at_x(1), 1, :, :, self.b], xm),
            )
            for copy in self.ay1:
                copy.wait_recv()
            self.ay2 = (
                go.send(self.ra.at[0], gb.at[:, at_y(-1) // 2, 0, :, self.a], yp),
                go.send(self.ra.at[1], gb.at[:, at_y(1) // 2, 1, :, self.a], ym),
            )

        def fifth(self):
            for copy in self.bx2 + self.ay2:
                copy.wait_recv()

    def weight_grad(s0, n):
        block = gb[:, :, :, :, 64 * s0:64 * (s0 + n)].reshape(512, 64 * n)
        wg[s0:s0 + n] = dot_tn(block, att[...]).astype(BF16).reshape(n, 2, 32, 512)
        rows_n = pl.ds(s0, n)
        return go.send(wg.at[rows_n, 1 - c], wgr.at[rows_n], mate)

    def own_chunk(rel):
        return wg[slot(rel), c].astype(F32) + wgr[slot(rel)].astype(F32)

    chains = ((8, 4), (7, 4), (-7, 4), (-6, 3))
    came = [None] * 4

    def chain_step(m):
        for n, (first, length) in enumerate(chains):
            if m >= length:
                continue
            sign = 1 if first > 0 else -1
            dist = first - 2 * sign * m
            value = own_chunk(dist)
            if m > 0:
                came[n].wait_recv()
                value = value + zrecv[n, m - 1].astype(F32)
            zsend[n, m] = value.astype(BF16)
            device = {2: zp2, 1: zp, -1: zm, -2: zm2}[max(-2, min(2, dist))]
            came[n] = go.send(zsend.at[n, m], zrecv.at[n, m], device)

    spread_far = Spread(2, 640, 768, 128)
    spread_mid = Spread(1, 512, 896, 128)
    spread_far.second()
    spread_mid.second()
    spread_far.third()
    spread_mid.third()
    spread_near = Spread(0, 0, 256, 256)
    spread_far.fourth()
    spread_mid.fourth()
    spread_near.second()
    spread_far.fifth()
    wg_far = weight_grad(10, 4)
    spread_mid.fifth()
    wg_mid = (weight_grad(8, 2), weight_grad(14, 2))
    spread_near.third()
    wg_far.wait_recv()
    chain_step(0)
    spread_near.fourth()
    for copy in wg_mid:
        copy.wait_recv()
    chain_step(1)
    spread_near.fifth()
    wg_near = (weight_grad(0, 4), weight_grad(4, 4))

    for j in range(2):
        total = None
        for zz in range(4):
            term = dot(
                gb[:, :, :, :, 256 * zz:256 * zz + 256].reshape(512, 256),
                proj[4 * zz:4 * zz + 4, :, :, 256 * j:256 * j + 256].reshape(256, 256),
            )
            total = term if total is None else total + term
        ga[:, 256 * j:256 * j + 256] = total.astype(BF16)

    for i in range(4):
        b_own[i] = dot_tn(q_ref[:, hs(i)], ga[:, hs(i)]).astype(BF16)
    back_copy = go.send(b_own, b_recv, mate)

    def backward(i):
        q0_, q1_ = q_ref[top, hs(i)], q_ref[bot, hs(i)]
        k0_, k1_ = k_ref[top, hs(i)], k_ref[bot, hs(i)]
        v0_, v1_ = v_ref[top, hs(i)], v_ref[bot, hs(i)]
        a0_, a1_ = ga[top, hs(i)], ga[bot, hs(i)]
        m00, m10, m11 = scores_of(ga, v_ref, i)
        e, b = s_in[i], b_in[i]
        gq_ref[top, hs(i)] = (scale * (dot(m00, k0_) + dot_nt(a0_, e))).astype(BF16)
        gq_ref[bot, hs(i)] = (
            scale * (dot(m10, k0_) + dot(m11, k1_) + dot_nt(a1_, e))
        ).astype(BF16)
        gk_ref[top, hs(i)] = (
            scale * (dot_tn(m00, q0_) + dot_tn(m10, q1_) + dot_nt(v0_, b))
        ).astype(BF16)
        gk_ref[bot, hs(i)] = (scale * (dot_tn(m11, q1_) + dot_nt(v1_, b))).astype(BF16)
        gv_ref[top, hs(i)] = (
            scale * (dot_tn(sc[i, 0], a0_) + dot_tn(sc[i, 1], a1_) + dot(k0_, b))
        ).astype(BF16)
        gv_ref[bot, hs(i)] = (scale * (dot_tn(sc[i, 2], a1_) + dot(k1_, b))).astype(BF16)

    back_copy.wait_recv()
    bt_own[...] = (b_own[...].astype(F32) + b_recv[...].astype(F32)).astype(BF16)
    back_pair = go.send(bt_own, bt_recv, pair)
    for copy in wg_near:
        copy.wait_recv()
    chain_step(2)
    chain_step(3)
    back_pair.wait_recv()
    b_in[...] = (
        (1.0 - cf) * b_recv[...].astype(F32) + (1.0 - ylf) * bt_recv[...].astype(F32)
    ).astype(BF16)
    backward(0)
    backward(1)
    total = own_chunk(0)
    for n, (first, length) in enumerate(chains):
        came[n].wait_recv()
        total = total + zrecv[n, length - 1].astype(F32)
    y_own[...] = total.astype(BF16)
    last = [go.send(y_own, y_recv.at[n], device) for n, device in enumerate((pair, mate, cross))]
    backward(2)
    backward(3)
    for copy in last:
        copy.wait_recv()
    go_ref[pl.ds(pl.multiple_of(mine, 32), 32), :] = (
        y_own[...].astype(F32) + y_recv[0].astype(F32)
    )
    go_ref[pl.ds(pl.multiple_of(32 - mine, 32), 32), :] = (
        y_recv[1].astype(F32) + y_recv[2].astype(F32)
    )
    go.drain()


def out_kernel(*refs):
    copies = [
        pltpu.make_async_copy(refs[n], refs[4 + n], refs[8].at[n]) for n in range(4)
    ]
    for copy in copies:
        copy.start()
    for copy in copies:
        copy.wait()


def write_out(*arrays):
    return pl.pallas_call(
        out_kernel,
        out_shape=tuple(jax.ShapeDtypeStruct(a.shape, a.dtype) for a in arrays),
        in_specs=[pl.BlockSpec(memory_space=pltpu.VMEM)] * 4,
        out_specs=(pl.BlockSpec(memory_space=pltpu.HBM),) * 4,
        scratch_shapes=[pltpu.SemaphoreType.DMA((4,))],
        compiler_params=pltpu.CompilerParams(vmem_limit_bytes=8 * 1024 * 1024),
        name="write_out",
    )(*arrays)


def on_device(queries, keys, values, out_proj, depth_proj, code_table, code_ids, depth_cotangent):
    scale = 2048.0 ** (-0.5)
    def vm(shape, kind=BF16):
        return pltpu.VMEM(shape, kind)

    state = vm((4, DH, DH))
    gq, gk, gv, gop = pl.pallas_call(
        functools.partial(kernel, scale),
        out_shape=(
            jax.ShapeDtypeStruct((512, 512), BF16),
            jax.ShapeDtypeStruct((512, 512), BF16),
            jax.ShapeDtypeStruct((512, 512), BF16),
            jax.ShapeDtypeStruct((64, 512), F32),
        ),
        in_specs=[pl.BlockSpec(memory_space=pltpu.HBM)] * 8,
        out_specs=(pl.BlockSpec(memory_space=pltpu.VMEM),) * 4,
        scratch_shapes=[
            vm((512, 512)), vm((512, 512)), vm((512, 512)), vm((64, 512)),
            vm((8, 1024)), vm((2, 8, 1024)), vm((2, 64), jnp.int32), vm((64, 2, 1024)),
            pltpu.SemaphoreType.DMA((8,)),
            vm((16, 3, 16, 128)), vm((16, 2, 32, 512)), vm((3, 4, 2, 2, 64, 1024)),
            state, state, state, state, state,
            state, state, state, state, state,
            vm((4, 3, 256, 256)), vm((512, 512), F32), vm((512, 512)),
            vm((4, 2, 2, 32, 1024)),
            vm((3, 2, 32, 256)), vm((3, 2, 32, 256)),
            vm((3, 2, 2, 32, 256)), vm((3, 2, 2, 32, 256)),
            vm((3, 2, 32, 256)), vm((3, 2, 32, 256)), vm((3, 2, 32, 256)),
            vm((3, 2, 4, 32, 256)), vm((3, 2, 4, 32, 256)),
            vm((3, 4, 2, 32, 256)), vm((3, 2, 32, 256)), vm((3, 2, 2, 32, 256)),
            vm((64, 1024), F32), vm((2, 64, 1024), F32), vm((64, 1024), F32),
            vm((4, 2, 2, 32, 1024)), vm((3, 2, 4, 32, 256)), vm((3, 2, 32, 256)),
            vm((512, 512)), vm((16, 2, 32, 512)), vm((16, 32, 512)),
            vm((4, 4, 32, 512)), vm((4, 4, 32, 512)),
            vm((32, 512)), vm((3, 32, 512)),
            pltpu.SemaphoreType.DMA((N_COPIES,)),
            pltpu.SemaphoreType.DMA((N_COPIES,)),
        ],
        compiler_params=pltpu.CompilerParams(
            collective_id=0, has_side_effects=True, vmem_limit_bytes=34 * 1024 * 1024
        ),
        name="fused_step",
    )(
        *(
            pltpu.with_memory_space_constraint(array, pltpu.HBM)
            for array in (
                queries[0], keys[0], values[0], out_proj.T, depth_proj.T, code_table,
                code_ids[0].T, depth_cotangent[0],
            )
        )
    )
    gq, gk, gv, gop = write_out(gq, gk, gv, gop)
    return gq[None], gk[None], gv[None], gop.T


def solution(mesh):
    in_specs = (
        P("dp", "seq", "head"),
        P("dp", "seq", "head"),
        P("dp", "seq", "head"),
        P("head", "dp"),
        P(None, ("head", "dp")),
        P(None, ("head", "dp"), None),
        P("dp", ("seq", "head"), None),
        P("dp", ("seq", "head"), None, None),
    )
    out_specs = (
        P("dp", "seq", "head"),
        P("dp", "seq", "head"),
        P("dp", "seq", "head"),
        P("head", "dp"),
    )
    return jax.shard_map(
        on_device, mesh=mesh, in_specs=in_specs, out_specs=out_specs, check_vma=False
    )
```
